32 devices in a mesh: clip: 2 (over y), tile: 4 (over z), slab: 2 (over x), chan: 2 (over core).
Axes of the slice: x: 2, y: 2, z: 4, core: 2. Of those that a mesh axis runs over, the one named last changes fastest.
Arguments:
- video: bfloat16 [16, 16, 128, 128], P(('clip', 'slab'), 'tile'), parts along dimension 0, may hold values from -6 to 6
- first_weight: bfloat16 [3, 3, 3, 128, 128], P(None, None, None, None, 'chan'), may hold values from -0.109375 to 0.109375
- first_bias: float32 [128], P('chan'), may hold values from -3 to 3
- second_weight: bfloat16 [3, 3, 3, 128, 256], replicated, may hold values from -0.109375 to 0.109375
- second_bias: float32 [256], P('chan'), may hold values from -3 to 3
Outputs:
- latents: bfloat16 [8, 16, 128, 256], P(('clip', 'slab'), 'tile', None, 'chan'), parts along dimension 0
The draws below stay inside these ranges and needn't reach their ends.
There are 2 independent parts, one for each index of `clip`. The reference program is written for one: setup_inputs(seed, part) draws one part's arguments, and reference() takes and returns one part's arrays. A program takes and returns all parts, laid end to end along the dimension named above; an argument that names none is the same for every part. Nothing has to cross between parts.
All inputs are finite; a program needn't handle non-finite values.
Results may differ from the reference program's by a relative error of at most 0.0095.
Values may be sent and summed in bfloat16 or wider, within the bound.
A program may use at most 64 MiB of HBM per device.

```python
import jax
import jax.numpy as jnp
from jax import lax

CH_IN = 128
CH_MID = 128
CH_OUT = 256
W = 128
FRAMES = 8
HEIGHT = 16


def level_of(stream_key, shape, cuts, smallest, largest):
    def one(dim, parts):
        heights = jax.random.uniform(jax.random.fold_in(jax.random.fold_in(stream_key, 6), dim), (parts,), jnp.float32, smallest / len(cuts), largest / len(cuts))
        return jnp.repeat(jnp.exp(heights), shape[dim] // parts).reshape((-1,) + (1,) * (len(shape) - dim - 1))

    level = one(*cuts[0])
    for cut in cuts[1:]:
        level = level * one(*cut)
    return level


def scatter_about(rng, shape, spread, limit, shards=(), dtype=jnp.bfloat16):
    factor_of = level_of(rng, shape, shards, -0.22, 0.18) if shards else 1.0
    entries = jax.random.normal(rng, shape, jnp.float32) * spread * factor_of
    return jnp.minimum(jnp.maximum(entries, -limit), limit).astype(dtype)


def setup_inputs(seed: int = 0, part: int = 0) -> dict:
    arg_keys = jax.random.split(jax.random.key(seed), 6)
    part_keys = jax.random.split(jax.random.fold_in(arg_keys[5], part), 6)
    video = scatter_about(part_keys[0], (FRAMES, HEIGHT, W, CH_IN), 1.0, 6.0, ((0, 2), (1, 4)))
    first_weight = scatter_about(arg_keys[1], (3, 3, 3, CH_IN, CH_MID), (27 * CH_IN) ** -0.5, 0.109375, ((4, 2),))
    first_bias = scatter_about(arg_keys[2], (CH_MID,), 0.5, 3.0, ((0, 2),), jnp.float32)
    second_weight = scatter_about(arg_keys[3], (3, 3, 3, CH_MID, CH_OUT), (27 * CH_MID) ** -0.5, 0.109375)
    second_bias = scatter_about(arg_keys[4], (CH_OUT,), 0.5, 3.0, ((0, 2),), jnp.float32)
    return {"video": video, "first_weight": first_weight, "first_bias": first_bias, "second_weight": second_weight, "second_bias": second_bias}


def causal_convolve(source, kernel, stride):
    result = lax.conv_general_dilated(source[None], kernel, window_strides=(stride, 1, 1), padding=((2, 0), (1, 1), (1, 1)), dimension_numbers=("NDHWC", "DHWIO", "NDHWC"), preferred_element_type=jnp.float32)
    return result[0]


def reference(video, first_weight, first_bias, second_weight, second_bias):
    hidden = jax.nn.silu(causal_convolve(video, first_weight, 1) + first_bias).astype(jnp.bfloat16)
    return jax.nn.silu(causal_convolve(hidden, second_weight, 2) + second_bias).astype(jnp.bfloat16)
```

```python
import functools

import jax
import jax.numpy as jnp
from jax import lax
from jax.experimental import pallas as pl
from jax.experimental.pallas import tpu as pltpu
from jax.sharding import PartitionSpec as P

MESH = pl.DeviceIdType.MESH
BACK = 2


def kernel(
    tiles, slabs, video, w1, b1, w2, b2, out,
    v, h, k1, k2, bias1, bias2, pieces, incoming, going, going0, sum0, acc,
    load, w1_s, w1_r, b_s, b_r, x_s, x_r, z_s, z_r, p_s, p_r, f_s, f_r, q_s, q_r, o_s, o_r,
):
    frames, rows, columns, channels = video.shape
    half = rows // 2
    width = b2.shape[1]
    core = lax.axis_index("chan")
    tile = lax.axis_index("tile")
    slab = lax.axis_index("slab")
    other = 1 - core
    z_tile = tile + 2 * core - 1
    has_z = jnp.logical_and(z_tile >= 0, z_tile < tiles)
    no_z = jnp.logical_or(z_tile < 0, z_tile >= tiles)
    has_next = slab < slabs - 1
    no_next = slab == slabs - 1
    has_prev = slab > 0
    no_prev = slab == 0
    peer = {"chan": other}
    z_peer = {"chan": other, "tile": z_tile}
    next_same = {"slab": slab + 1}
    next_cross = {"slab": slab + 1, "chan": other}
    prev_same = {"slab": slab - 1}
    prev_cross = {"slab": slab - 1, "chan": other}

    def when(condition, body):
        if condition is None:
            body()
        else:
            pl.when(condition)(body)

    barrier = pltpu.get_barrier_semaphore()
    everyone = (
        (None, peer), (has_z, z_peer), (has_next, next_same), (has_next, next_cross),
        (has_prev, prev_same), (has_prev, prev_cross),
    )
    for condition, device in everyone:
        when(condition, lambda device=device: pl.semaphore_signal(
            barrier, inc=1, device_id=device, device_id_type=MESH))
    met = 1 + sum(jnp.where(condition, 1, 0) for condition, _ in everyone[1:])

    into_v = pltpu.make_async_copy(video, v.at[pl.ds(BACK, frames), pl.ds(half * other, rows)], load.at[0])
    own_w1 = pltpu.make_async_copy(w1, k1.at[:, :, core], load.at[1])
    own_b1 = pltpu.make_async_copy(b1, bias1.at[core], load.at[2])
    own_b2 = pltpu.make_async_copy(b2, bias2.at[0], load.at[3])
    own_w2 = [
        pltpu.make_async_copy(
            w2.at[:, :, :, pl.ds(pl.multiple_of(owner * width, width), width)], k2.at[n], load.at[4 + n])
        for n, owner in enumerate((core, other))
    ]
    for copy in (into_v, own_w1, own_b1, own_b2):
        copy.start()

    def remote(src, dst, send, recv, device):
        return pltpu.make_async_remote_copy(
            src_ref=src, dst_ref=dst, send_sem=send, recv_sem=recv,
            device_id=device, device_id_type=MESH,
        )

    mine = pl.ds(half * core, half)
    theirs = pl.ds(half * other, half)
    arrived = pl.ds(half, half)
    halo_here = pl.ds(rows * core, half)
    halo_there = pl.ds(rows * other, half)
    inner_here = pl.ds(rows * other, half)
    inner_there = pl.ds(rows * core, half)
    early_frames = pl.ds(BACK, frames - 1)
    late_frame = pl.ds(BACK + frames - 1, 1)
    near_here = pl.ds(1 + (rows - 1) * core, 1)
    near_there = pl.ds(1 + (rows - 1) * other, 1)
    far_here = pl.ds((rows + 1) * core, 1)
    far_there = pl.ds((rows + 1) * other, 1)
    near_row = pl.ds((rows - 1) * core, 1)
    far_row = pl.ds(half - 1 + core, 1)

    to_next = [
        remote(video.at[frames - BACK + f, theirs], v.at[f, arrived], x_s.at[f], x_r.at[f], next_cross)
        for f in range(BACK)
    ]

    def z_copies(near, far):
        return [
            remote(video.at[pl.ds(0, frames - 1), near[0]], v.at[early_frames, near[1]], z_s.at[0], z_r.at[0], z_peer),
            remote(video.at[pl.ds(frames - 1, 1), near[0]], v.at[late_frame, near[1]], z_s.at[1], z_r.at[1], z_peer),
            remote(video.at[pl.ds(0, frames - 1), far[0]], v.at[early_frames, far[1]], z_s.at[2], z_r.at[2], z_peer),
            remote(video.at[pl.ds(frames - 1, 1), far[0]], v.at[late_frame, far[1]], z_s.at[3], z_r.at[3], z_peer),
        ]

    z_out = z_copies((near_row, near_there), (far_row, far_there))
    z_in = z_copies((near_row, near_here), (far_row, far_here))
    forward_p = [
        remote(v.at[f, arrived], v.at[f, inner_there], p_s.at[f], p_r.at[f], peer) for f in range(BACK)
    ]
    forward_z = [
        remote(v.at[f, arrived], v.at[f, halo_there], f_s.at[f], f_r.at[f], z_peer) for f in range(BACK)
    ]
    to_peer = [
        remote(w1, k1.at[:, :, core], w1_s, w1_r, peer),
        remote(b1, bias1.at[core], b_s.at[0], b_r.at[0], peer),
        remote(b2, bias2.at[1], b_s.at[1], b_r.at[1], peer),
    ]

    with jax.named_scope("entrybar"):
        pl.semaphore_wait(barrier, met)

    @pl.when(has_next)
    def _():
        to_next[1].start()

    @pl.when(has_z)
    def _():
        z_out[0].start()

    @pl.when(jnp.logical_and(has_z, has_next))
    def _():
        z_out[1].start()

    to_peer[0].start()

    @pl.when(has_next)
    def _():
        to_next[0].start()

    @pl.when(has_z)
    def _():
        z_out[2].start()

    @pl.when(jnp.logical_and(has_z, has_next))
    def _():
        z_out[3].start()

    to_peer[1].start()
    to_peer[2].start()
    for copy in own_w2:
        copy.start()

    @pl.when(no_z)
    def _():
        v[:, halo_here] = jnp.zeros((v.shape[0], half, columns, channels), v.dtype)

    def taps(source, index, first, count, steps):
        return jnp.concatenate(
            [
                source[index + a, pl.ds(first + b, count)].reshape(count * columns, channels)
                for a in steps
                for b in range(3)
            ],
            axis=1,
        )

    def shifted(parts, size):
        column = lax.broadcasted_iota(jnp.int32, (parts.shape[0], size), 0) % columns
        before = pltpu.roll(parts[:, 0:size], 1, 0)
        after = pltpu.roll(parts[:, 2 * size : 3 * size], parts.shape[0] - 1, 0)
        total = parts[:, size : 2 * size] + jnp.where(column == 0, 0.0, before)
        return total + jnp.where(column == columns - 1, 0.0, after)

    def silu(total):
        return total / (1.0 + jnp.exp(-total))

    def hidden(indices, first, count, oldest=0):
        parts = lax.dot_general(
            jnp.concatenate([taps(v, index - 2, first, count, range(oldest, 3)) for index in indices], axis=0),
            jnp.concatenate([k1[tap].reshape(3 * channels, channels) for tap in range(3 * oldest, 9)], axis=1),
            (((1,), (1,)), ((), ())),
            preferred_element_type=jnp.float32,
        )
        bias = jnp.concatenate([bias1[0], bias1[1]], axis=1)
        value = silu(shifted(parts, channels) + bias).astype(h.dtype)
        value = value.reshape(len(indices), count, columns, channels)
        for n, index in enumerate(indices):
            h[index, pl.ds(first, count)] = value[n]

    def inner(*indices, oldest=0):
        with jax.named_scope("inner" + "_".join(map(str, indices))):
            hidden(indices, half * other, half, oldest)

    def clear_outside(index):
        @pl.when(no_z)
        def _():
            h[index, pl.ds((rows - 1) * core, 1)] = jnp.zeros((1, columns, channels), h.dtype)

    def outer(*indices, oldest=0):
        with jax.named_scope("outer" + "_".join(map(str, indices))):
            hidden(indices, half * core, half, oldest)
            for index in indices:
                clear_outside(index)

    def near(*indices):
        with jax.named_scope("near"):
            hidden(indices, 1 + core, 1)

    def far(*indices):
        with jax.named_scope("far"):

            @pl.when(has_z)
            def _():
                hidden(indices, (rows - 1) * core, 1)

            for index in indices:
                clear_outside(index)

    def second(index, first, count, steps):
        matrix = jnp.concatenate(
            [
                jnp.concatenate([k2[n, 3 * a + b, e] for e in range(3) for n in range(2)], axis=1)
                for a in steps
                for b in range(3)
            ],
            axis=0,
        )
        parts = jnp.dot(taps(h, index, first, count, steps), matrix, preferred_element_type=jnp.float32)
        return [
            shifted(
                jnp.concatenate(
                    [parts[:, (2 * e + n) * width : (2 * e + n + 1) * width] for e in range(3)], axis=1
                ),
                width,
            )
            for n in range(2)
        ]

    def share(slot, local):
        place = half * core + local
        return [
            remote(pieces.at[slot, 0], incoming.at[place], q_s.at[2 * slot], q_r.at[place], next_same),
            remote(pieces.at[slot, 1], incoming.at[place], q_s.at[2 * slot + 1], q_r.at[place], next_cross),
        ]

    shares = [share(0, other), share(1, core)]

    def send_share(slot, local):
        with jax.named_scope("share%d" % slot):
            both = second(frames, local, 1, range(0, 2))
            for n in (1, 0):
                pieces[slot, n] = both[n].astype(pieces.dtype)
                shares[slot][n].start()

    result = [
        remote(going.at[t - 1], out.at[t, mine], o_s.at[t], o_r.at[t], peer) for t in range(1, frames // 2)
    ]
    part0 = remote(going0, sum0.at[mine], o_s.at[0], o_r.at[0], peer)

    def finish(t, both):
        going[t - 1] = silu(both[1] + bias2[1]).astype(out.dtype).reshape(half, columns, width)
        result[t - 1].start()
        out[t, mine] = silu(both[0] + bias2[0]).astype(out.dtype).reshape(half, columns, width)

    def latent(t):
        with jax.named_scope("latent%d" % t):
            finish(t, second(2 * t, 0, half, range(3)))

    def first_latent():
        with jax.named_scope("latent0"):
            both = second(0, 0, half, range(2, 3))
            going0[...] = both[1].reshape(half, columns, width)
            part0.start()
            sum0[mine] = both[0].reshape(half, columns, width)

    def wait_z(which):
        with jax.named_scope("zwait%d" % which):

            @pl.when(has_z)
            def _():
                z_in[which].wait_recv()

    def pass_on(f):
        with jax.named_scope("pass%d" % f):

            @pl.when(has_prev)
            def _():
                remote(
                    video.at[frames - BACK + f, theirs], v.at[f, arrived], x_s.at[f], x_r.at[f], prev_cross
                ).wait_recv()
                forward_p[f].start()

                @pl.when(has_z)
                def _():
                    forward_z[f].start()

    def inner_ready(f):
        with jax.named_scope("pwait%d" % f):
            remote(v.at[f, arrived], v.at[f, inner_here], p_s.at[f], p_r.at[f], peer).wait_recv()

    def outer_ready(f):
        with jax.named_scope("fwait%d" % f):

            @pl.when(has_z)
            def _():
                remote(v.at[f, arrived], v.at[f, halo_here], f_s.at[f], f_r.at[f], z_peer).wait_recv()

    with jax.named_scope("loadwait"):
        into_v.wait()
        own_w1.wait()
        own_b1.wait()
        own_b2.wait()
    with jax.named_scope("w1wait"):
        remote(w1, k1.at[:, :, other], w1_s, w1_r, peer).wait_recv()
        remote(b1, bias1.at[other], b_s.at[0], b_r.at[0], peer).wait_recv()
        to_peer[2].wait_recv()

    last = frames + 1

    @pl.when(has_next)
    def _():
        inner(frames, last)

    @pl.when(no_next)
    def _():
        inner(frames)

    @pl.when(no_prev)
    def _():
        inner(3, oldest=1)
        inner(2, oldest=2)

    pass_on(1)
    wait_z(0)

    @pl.when(has_next)
    def _():
        wait_z(1)
        near(frames, last)
        with jax.named_scope("w2wait"):
            for copy in own_w2:
                copy.wait()
        send_share(0, other)

    wait_z(2)

    @pl.when(no_next)
    def _():
        outer(frames)
        with jax.named_scope("w2wait"):
            for copy in own_w2:
                copy.wait()

    pass_on(0)

    @pl.when(has_next)
    def _():
        wait_z(3)
        far(frames, last)
        send_share(1, core)

    for index in range(frames - 1, 3, -1):
        inner(index)
        outer(index)
    for t in range(2, frames // 2):
        latent(t)

    @pl.when(no_prev)
    def _():
        outer(3, oldest=1)
        outer(2, oldest=2)
        first_latent()
        latent(1)

    @pl.when(has_prev)
    def _():
        inner_ready(1)
        inner(3)
        inner_ready(0)
        inner(2)
        outer_ready(1)
        outer(3)
        with jax.named_scope("latent1a"):
            both = second(2, 0, half, range(1, 3))
            for n in range(2):
                acc[n] = both[n]
        outer_ready(0)
        outer(2)
        first_latent()
        with jax.named_scope("latent1b"):
            both = second(2, 0, half, range(0, 1))
            finish(1, [acc[n] + both[n] for n in range(2)])

    with jax.named_scope("part0"):
        remote(going0, sum0.at[theirs], o_s.at[0], o_r.at[0], peer).wait_recv()

    def close(first, count, extra):
        total = sum0[pl.ds(first, count)].reshape(count * columns, width)
        if extra:
            total = total + incoming[pl.ds(first, count)].reshape(count * columns, width).astype(jnp.float32)
        out[0, pl.ds(first, count)] = silu(total + bias2[0]).astype(out.dtype).reshape(count, columns, width)

    @pl.when(has_prev)
    def _():
        for row in (1, 2, 0, 3):
            with jax.named_scope("close%d" % row):
                remote(pieces.at[0, 0], incoming.at[row], q_s.at[0], q_r.at[row], prev_same).wait_recv()
                close(row, 1, True)

    @pl.when(no_prev)
    def _():
        close(0, rows, False)

    with jax.named_scope("ends"):
        for copy in to_peer:
            copy.wait_send()
        part0.wait_send()
        for t in range(1, frames // 2):
            remote(going.at[t - 1], out.at[t, theirs], o_s.at[t], o_r.at[t], peer).wait_recv()
            result[t - 1].wait_send()

        @pl.when(has_next)
        def _():
            for copy in to_next + shares[0] + shares[1]:
                copy.wait_send()

        @pl.when(has_z)
        def _():
            z_out[0].wait_send()
            z_out[2].wait_send()

        @pl.when(jnp.logical_and(has_z, has_next))
        def _():
            z_out[1].wait_send()
            z_out[3].wait_send()

        @pl.when(has_prev)
        def _():
            for copy in forward_p:
                copy.wait_send()

        @pl.when(jnp.logical_and(has_prev, has_z))
        def _():
            for copy in forward_z:
                copy.wait_send()


def shards(tiles, slabs, video, first_weight, first_bias, second_weight, second_bias):
    frames, rows, columns, channels = video.shape
    half = rows // 2
    assert half == 2 and frames >= 4 and frames % 2 == 0
    part = first_bias.shape[0]
    width = second_bias.shape[0]
    anywhere = pl.BlockSpec(memory_space=pltpu.HBM)
    inside = pl.BlockSpec(memory_space=pltpu.VMEM)
    dma = pltpu.SemaphoreType.DMA
    vmem = pltpu.VMEM
    latents = frames // 2
    return pl.pallas_call(
        functools.partial(kernel, tiles, slabs),
        out_shape=jax.ShapeDtypeStruct((latents, rows, columns, width), jnp.bfloat16),
        in_specs=[anywhere] * 5,
        out_specs=inside,
        scratch_shapes=[
            vmem((BACK + frames, rows + 2, columns, channels), jnp.bfloat16),
            vmem((frames + 2, half + 2, columns, channels), jnp.bfloat16),
            vmem((9, 3, 2, part, channels), jnp.bfloat16),
            vmem((2, 9, 3, channels, width), jnp.bfloat16),
            vmem((2, 1, part), jnp.float32),
            vmem((2, 1, width), jnp.float32),
            vmem((2, 2, columns, width), jnp.bfloat16),
            vmem((rows, columns, width), jnp.bfloat16),
            vmem((latents - 1, half, columns, width), jnp.bfloat16),
            vmem((half, columns, width), jnp.float32),
            vmem((rows, columns, width), jnp.float32),
            vmem((2, half * columns, width), jnp.float32),
            dma((6,)), dma, dma, dma((2,)), dma((2,)), dma((BACK,)), dma((BACK,)), dma((4,)), dma((4,)),
            dma((BACK,)), dma((BACK,)), dma((BACK,)), dma((BACK,)), dma((4,)), dma((rows,)),
            dma((latents,)), dma((latents,)),
        ],
        compiler_params=pltpu.CompilerParams(
            collective_id=0, has_side_effects=True, vmem_limit_bytes=32 << 20
        ),
    )(
        *(
            pltpu.with_memory_space_constraint(operand, pltpu.HBM)
            for operand in (
                video,
                jnp.swapaxes(first_weight, 3, 4).reshape(9, 3, part, channels),
                first_bias.reshape(1, part),
                second_weight.reshape(9, 3, channels, 2 * width),
                second_bias.reshape(1, width),
            )
        )
    )


def solution(mesh):
    placed = (
        P(("clip", "slab"), "tile", None, None),
        P(None, None, None, None, "chan"),
        P("chan"),
        P(),
        P("chan"),
    )
    return jax.shard_map(
        functools.partial(shards, mesh.shape["tile"], mesh.shape["slab"]),
        mesh=mesh,
        in_specs=placed,
        out_specs=P(("clip", "slab"), "tile", None, "chan"),
        check_vma=False,
    )
```

```python
import functools

import jax
import jax.numpy as jnp
from jax import lax
from jax.experimental import pallas as pl
from jax.experimental.pallas import tpu as pltpu
from jax.sharding import PartitionSpec as P

MESH = pl.DeviceIdType.MESH
BACK = 2


def kernel(
    tiles, slabs, video, w1, b1, w2, b2, out,
    v, h, k1, k2, bias1, bias2, pieces, incoming, going, going0, sum0, acc,
    load, w_s, b_s, x_s, z_s, p_s, q_s, o_s, w1_r, b_r, x_r, z_r, p_r, h_r, f_r, q_r, o_r,
):
    frames, rows, columns, channels = video.shape
    half = rows // 2
    width = b2.shape[1]
    core = lax.axis_index("chan")
    tile = lax.axis_index("tile")
    slab = lax.axis_index("slab")
    other = 1 - core
    z_tile = tile + 2 * core - 1
    has_z = jnp.logical_and(z_tile >= 0, z_tile < tiles)
    no_z = jnp.logical_or(z_tile < 0, z_tile >= tiles)
    has_next = slab < slabs - 1
    no_next = slab == slabs - 1
    has_prev = slab > 0
    no_prev = slab == 0
    one = core == 1
    zero = core == 0
    above = tile > 0
    below = tile < tiles - 1
    peer = {"chan": other}
    z_minus = {"tile": tile - 1, "chan": 1}
    z_plus = {"tile": tile + 1, "chan": 0}
    next_same = {"slab": slab + 1}
    next_cross = {"slab": slab + 1, "chan": other}
    prev_same = {"slab": slab - 1}

    def both(*conditions):
        return functools.reduce(jnp.logical_and, conditions)

    def when(condition, body):
        if condition is None:
            body()
        else:
            pl.when(condition)(body)

    barrier = pltpu.get_barrier_semaphore()
    greetings = (
        (None, peer),
        (has_z, {"chan": other, "tile": z_tile}),
        (has_prev, {"slab": slab - 1, "chan": 1}),
    )
    for condition, device in greetings:
        when(condition, lambda device=device: pl.semaphore_signal(
            barrier, inc=1, device_id=device, device_id_type=MESH))
    met = 1
    for condition, count in ((has_z, 1), (both(one, has_next), 2)):
        met = met + jnp.where(condition, count, 0)

    into_v = pltpu.make_async_copy(video, v.at[pl.ds(BACK, frames), pl.ds(half * other, rows)], load.at[0])
    own_w1 = pltpu.make_async_copy(w1, k1.at[:, :, core], load.at[1])
    own_b1 = pltpu.make_async_copy(b1, bias1.at[core], load.at[2])
    own_b2 = pltpu.make_async_copy(b2, bias2.at[0], load.at[4])
    own_w2 = [
        pltpu.make_async_copy(
            w2.at[:, :, :, pl.ds(pl.multiple_of(owner * width, width), width)], k2.at[n], load.at[3])
        for n, owner in enumerate((core, other))
    ]
    for copy in (into_v, own_w1, own_b1, own_b2):
        copy.start()

    def remote(src, dst, send, recv, device):
        return pltpu.make_async_remote_copy(
            src_ref=src, dst_ref=dst, send_sem=send, recv_sem=recv,
            device_id=device, device_id_type=MESH,
        )

    def wait_bytes(ref, semaphore):
        pltpu.make_async_copy(ref, ref, semaphore).wait()

    mine = pl.ds(half * core, half)
    theirs = pl.ds(half * other, half)
    halo_here = pl.ds(rows * core, half)
    frame0, frame1 = frames, frames + 1

    low, high = pl.ds(0, half), pl.ds(half, half)
    halo_low, halo_high = pl.ds(0, half), pl.ds(rows, half)

    def x_copies(device):
        return [
            [
                remote(v.at[frames + f, some], v.at[f, some], x_s, x_r.at[2 * f + n], device)
                for n, some in enumerate((low, high))
            ]
            for f in range(BACK)
        ]

    x_out = x_copies(next_same)
    x_in = x_copies(prev_same)
    forward_z = [
        [
            (above, remote(v.at[f, low], v.at[f, halo_high], z_s.at[0], f_r.at[f], z_minus)),
            (below, remote(v.at[f, high], v.at[f, halo_low], z_s.at[1], f_r.at[f], z_plus)),
        ]
        for f in range(BACK)
    ]
    f_in = [remote(v.at[f, low], v.at[f, halo_low], z_s.at[0], f_r.at[f], peer) for f in range(BACK)]
    forward_p = [remote(v.at[f, low], v.at[f, pl.ds(half, half)], p_s, p_r.at[f], peer) for f in range(BACK)]
    forward_h = [
        remote(h.at[BACK + f, low], h.at[BACK + f, pl.ds(half, half)], p_s, h_r.at[f], peer) for f in range(BACK)
    ]

    def z_copies(count):
        some = pl.ds(BACK, count)
        return [
            [
                remote(video.at[pl.ds(0, count), pl.ds(n, 1)], v.at[some, pl.ds(rows + n, 1)], z_s.at[0], z_r.at[n], z_minus)
                for n in range(half)
            ],
            [
                remote(
                    v.at[some, pl.ds(rows - 1 - n, 1)], v.at[some, pl.ds(half - 1 - n, 1)], z_s.at[1], z_r.at[n], z_plus
                )
                for n in range(half)
            ],
        ]

    z_full = z_copies(frames)
    z_short = z_copies(frames - 1)

    def start_z(side):
        for condition, copies in ((has_next, z_full), (no_next, z_short)):

            @pl.when(condition)
            def _():
                for copy in copies[side]:
                    copy.start()

    to_peer = [
        remote(w1, k1.at[:, :, core], w_s, w1_r, peer),
        remote(b1, bias1.at[core], b_s.at[0], b_r.at[0], peer),
        remote(b2, bias2.at[1], b_s.at[1], b_r.at[1], peer),
    ]

    with jax.named_scope("entrybar"):
        pl.semaphore_wait(barrier, met)

    @pl.when(both(zero, above))
    def _():
        start_z(0)

    for copy in to_peer:
        copy.start()
    with jax.named_scope("loadwait"):
        into_v.wait()

    @pl.when(one)
    def _():
        @pl.when(has_next)
        def _():
            for n in range(2):
                for f in (1, 0):
                    x_out[f][n].start()

        @pl.when(below)
        def _():
            start_z(1)

    for copy in own_w2:
        copy.start()

    @pl.when(no_z)
    def _():
        v[:, halo_here] = jnp.zeros((v.shape[0], half, columns, channels), v.dtype)

    def taps(source, index, first, count, steps):
        return jnp.concatenate(
            [
                source[index + a, pl.ds(first + b, count)].reshape(count * columns, channels)
                for a in steps
                for b in range(3)
            ],
            axis=1,
        )

    def shifted(parts, size):
        column = lax.broadcasted_iota(jnp.int32, (parts.shape[0], size), 0) % columns
        before = pltpu.roll(parts[:, 0:size], 1, 0)
        after = pltpu.roll(parts[:, 2 * size : 3 * size], parts.shape[0] - 1, 0)
        total = parts[:, size : 2 * size] + jnp.where(column == 0, 0.0, before)
        return total + jnp.where(column == columns - 1, 0.0, after)

    def silu(total):
        return total / (1.0 + jnp.exp(-total))

    def hidden(indices, first, count, oldest=0):
        parts = lax.dot_general(
            jnp.concatenate([taps(v, index - 2, first, count, range(oldest, 3)) for index in indices], axis=0),
            jnp.concatenate([k1[tap].reshape(3 * channels, channels) for tap in range(3 * oldest, 9)], axis=1),
            (((1,), (1,)), ((), ())),
            preferred_element_type=jnp.float32,
        )
        bias = jnp.concatenate([bias1[0], bias1[1]], axis=1)
        value = silu(shifted(parts, channels) + bias).astype(h.dtype)
        value = value.reshape(len(indices), count, columns, channels)
        for n, index in enumerate(indices):
            h[index, pl.ds(first, count)] = value[n]

    def inner(*indices, oldest=0):
        with jax.named_scope("inner" + "_".join(map(str, indices))):
            hidden(indices, half * other, half, oldest)

    def clear_outside(index):
        @pl.when(no_z)
        def _():
            h[index, pl.ds((rows - 1) * core, 1)] = jnp.zeros((1, columns, channels), h.dtype)

    def outer(*indices, oldest=0):
        with jax.named_scope("outer" + "_".join(map(str, indices))):
            hidden(indices, half * core, half, oldest)
            for index in indices:
                clear_outside(index)

    def near(*indices):
        with jax.named_scope("near"):
            hidden(indices, 1 + core, 1)

    def far(*indices):
        with jax.named_scope("far"):

            @pl.when(has_z)
            def _():
                hidden(indices, (rows - 1) * core, 1)

            for index in indices:
                clear_outside(index)

    def second(index, first, count, steps, blocks):
        matrix = jnp.concatenate(
            [
                jnp.concatenate([k2[n, 3 * (a + shift) + b, e] for n, shift in blocks for e in range(3)], axis=1)
                for a in steps
                for b in range(3)
            ],
            axis=0,
        )
        parts = jnp.dot(taps(h, index, first, count, steps), matrix, preferred_element_type=jnp.float32)
        return [shifted(parts[:, 3 * k * width : 3 * (k + 1) * width], width) for k in range(len(blocks))]

    whole = ((0, 0), (1, 0))

    def share(slot, local):
        place = half * core + local
        return [
            remote(pieces.at[slot, 0], incoming.at[place], q_s, q_r.at[slot], next_same),
            remote(pieces.at[slot, 1], incoming.at[place], q_s, q_r.at[slot], next_cross),
        ]

    shares = [share(0, other), share(1, core)]

    def send_share(slot, local):
        with jax.named_scope("share%d" % slot):
            halves = second(frames, local, 1, range(0, 2), whole)
            for n in (1, 0):
                pieces[slot, n] = halves[n].astype(pieces.dtype)
                shares[slot][n].start()

    result = [
        remote(going.at[t - 1], out.at[t, mine], o_s, o_r.at[t], peer) for t in range(1, frames // 2)
    ]
    part0 = remote(going0, sum0.at[mine], o_s, o_r.at[0], peer)

    def latent(t):
        with jax.named_scope("latent%d" % t):
            own, away = second(2 * t, 0, half, range(3), whole)
            going[t - 1] = silu(away + bias2[1]).astype(out.dtype).reshape(half, columns, width)
            result[t - 1].start()
            out[t, mine] = silu(own + bias2[0]).astype(out.dtype).reshape(half, columns, width)

    def later_steps():
        with jax.named_scope("latent1a"):
            halves = second(2, 0, half, range(1, 3), whole)
            for n in range(2):
                acc[n] = halves[n]

    def last_steps():
        with jax.named_scope("tailA"):
            first, then = second(2, 0, half, range(0, 1), ((1, 2), (1, 0)))
            going0[...] = first.reshape(half, columns, width)
            part0.start()
            going[0] = silu(then + acc[1] + bias2[1]).astype(out.dtype).reshape(half, columns, width)
            result[0].start()
        with jax.named_scope("tailB"):
            first, then = second(2, 0, half, range(0, 1), ((0, 2), (0, 0)))
            sum0[mine] = first.reshape(half, columns, width)
            out[1, mine] = silu(then + acc[0] + bias2[0]).astype(out.dtype).reshape(half, columns, width)

    def wait_z(which, copies):
        with jax.named_scope("zwait%d" % which):

            @pl.when(has_z)
            def _():
                copies[0][which].wait_recv()

    def pass_on(f, n):
        with jax.named_scope("pass%d%d" % (f, n)):
            x_in[f][n].wait_recv()
            condition, copy = forward_z[f][n]
            pl.when(condition)(copy.start)
            if n == 0:
                forward_p[f].start()

    def from_peer(name, copy):
        @pl.when(zero)
        def _():
            with jax.named_scope(name):
                copy.wait_recv()

    def halo_ready(name, copy):
        with jax.named_scope(name):

            @pl.when(has_z)
            def _():
                copy.wait_recv()

    def w2_ready():
        with jax.named_scope("w2wait"):
            wait_bytes(k2, load.at[3])

    with jax.named_scope("loadwait"):
        own_w1.wait()
        own_b1.wait()
        own_b2.wait()
    with jax.named_scope("w1wait"):
        remote(w1, k1.at[:, :, other], w_s, w1_r, peer).wait_recv()
        remote(b1, bias1.at[other], b_s.at[0], b_r.at[0], peer).wait_recv()
        to_peer[2].wait_recv()

    last = frames + 1

    @pl.when(has_next)
    def _():
        inner(frames, last)

    @pl.when(no_next)
    def _():
        inner(frames)

    @pl.when(no_prev)
    def _():
        inner(3, oldest=1)
        inner(2, oldest=2)

    @pl.when(has_next)
    def _():
        wait_z(0, z_full)
        near(frames, last)
        w2_ready()

        send_share(0, other)
        wait_z(1, z_full)
        far(frames, last)
        send_share(1, core)

    def middle():
        for index in range(frames - 1, 3, -1):
            inner(index)
            outer(index)
        for t in range(2, frames // 2):
            latent(t)

    def own_last():
        @pl.when(no_next)
        def _():
            wait_z(0, z_short)
            wait_z(1, z_short)
            outer(frames)
            w2_ready()

    @pl.when(no_prev)
    def _():
        own_last()
        middle()
        outer(3, oldest=1)
        later_steps()
        outer(2, oldest=2)

    @pl.when(has_prev)
    def _():
        @pl.when(one)
        def _():
            pass_on(1, 0)
            pass_on(0, 0)
            pass_on(1, 1)
            inner(3)
            forward_h[1].start()
            pass_on(0, 1)
            inner(2)
            forward_h[0].start()

        own_last()
        middle()
        from_peer("pwait1", forward_p[1])
        halo_ready("fwait1", f_in[1])
        outer(3)
        from_peer("hwait1", forward_h[1])
        later_steps()
        from_peer("pwait0", forward_p[0])
        halo_ready("fwait0", f_in[0])
        outer(2)
        from_peer("hwait0", forward_h[0])

    last_steps()

    with jax.named_scope("part0"):
        remote(going0, sum0.at[theirs], o_s, o_r.at[0], peer).wait_recv()

    def close(first, count, extra):
        total = sum0[pl.ds(first, count)].reshape(count * columns, width)
        if extra:
            total = total + incoming[pl.ds(first, count)].reshape(count * columns, width).astype(jnp.float32)
        out[0, pl.ds(first, count)] = silu(total + bias2[0]).astype(out.dtype).reshape(count, columns, width)

    @pl.when(has_prev)
    def _():
        for slot, pair in enumerate(((half - 1, half), (0, rows - 1))):
            with jax.named_scope("close%d" % slot):
                wait_bytes(pieces.at[0], q_r.at[slot])
                for row in pair:
                    close(row, 1, True)

    @pl.when(no_prev)
    def _():
        close(0, rows, False)

    with jax.named_scope("ends"):
        for copy in to_peer:
            copy.wait_send()
        for t in range(1, frames // 2):
            remote(going.at[t - 1], out.at[t, theirs], o_s, o_r.at[t], peer).wait_recv()
        wait_bytes(v.at[pl.ds(0, frames // 2 + 1), low], o_s)

        @pl.when(has_next)
        def _():
            wait_bytes(incoming, q_s)

        @pl.when(both(one, has_next))
        def _():
            wait_bytes(v.at[pl.ds(0, BACK), pl.ds(0, rows)], x_s)

        @pl.when(both(one, has_prev))
        def _():
            wait_bytes(v.at[pl.ds(0, 2 * BACK), low], p_s)

        for side, condition in ((0, above), (1, below)):
            forwards = both(one, condition)
            for after, count in ((has_next, frames), (no_next, frames - 1)):
                if side == 0:

                    @pl.when(both(zero, condition, after))
                    def _():
                        wait_bytes(v.at[pl.ds(0, count), low], z_s.at[0])

                else:

                    @pl.when(both(forwards, after, no_prev))
                    def _():
                        wait_bytes(v.at[pl.ds(0, count), low], z_s.at[1])

                    @pl.when(both(forwards, after, has_prev))
                    def _():
                        wait_bytes(v.at[pl.ds(0, count + BACK), low], z_s.at[1])

            if side == 0:

                @pl.when(both(forwards, has_prev))
                def _():
                    wait_bytes(v.at[pl.ds(0, BACK), low], z_s.at[0])


def shards(tiles, slabs, video, first_weight, first_bias, second_weight, second_bias):
    frames, rows, columns, channels = video.shape
    half = rows // 2
    assert half == 2 and first_weight.shape[3] == channels == second_bias.shape[0] and frames >= 4 and frames % 2 == 0
    part = first_bias.shape[0]
    width = second_bias.shape[0]
    anywhere = pl.BlockSpec(memory_space=pltpu.HBM)
    inside = pl.BlockSpec(memory_space=pltpu.VMEM)
    dma = pltpu.SemaphoreType.DMA
    vmem = pltpu.VMEM
    latents = frames // 2
    return pl.pallas_call(
        functools.partial(kernel, tiles, slabs),
        out_shape=jax.ShapeDtypeStruct((latents, rows, columns, width), jnp.bfloat16),
        in_specs=[anywhere] * 5,
        out_specs=inside,
        scratch_shapes=[
            vmem((BACK + frames, rows + 2, columns, channels), jnp.bfloat16),
            vmem((frames + 2, half + 2, columns, channels), jnp.bfloat16),
            vmem((9, 3, 2, part, channels), jnp.bfloat16),
            vmem((2, 9, 3, channels, width), jnp.bfloat16),
            vmem((2, 1, part), jnp.float32),
            vmem((2, 1, width), jnp.float32),
            vmem((2, 2, columns, width), jnp.bfloat16),
            vmem((rows, columns, width), jnp.bfloat16),
            vmem((latents - 1, half, columns, width), jnp.bfloat16),
            vmem((half, columns, width), jnp.float32),
            vmem((rows, columns, width), jnp.float32),
            vmem((2, half * columns, width), jnp.float32),
            dma((5,)), dma, dma((2,)), dma, dma((2,)), dma, dma, dma, dma, dma((2,)), dma((2 * BACK,)), dma((2,)),
            dma((BACK,)), dma((BACK,)), dma((BACK,)), dma((2,)), dma((latents,)),
        ],
        compiler_params=pltpu.CompilerParams(
            collective_id=0, has_side_effects=True, vmem_limit_bytes=32 << 20
        ),
    )(
        *(
            pltpu.with_memory_space_constraint(operand, pltpu.HBM)
            for operand in (
                video,
                jnp.swapaxes(first_weight, 3, 4).reshape(9, 3, part, channels),
                first_bias.reshape(1, part),
                second_weight.reshape(9, 3, channels, 2 * width),
                second_bias.reshape(1, width),
            )
        )
    )


def solution(mesh):
    placed = (
        P(("clip", "slab"), "tile", None, None),
        P(None, None, None, None, "chan"),
        P("chan"),
        P(),
        P("chan"),
    )
    return jax.shard_map(
        functools.partial(shards, mesh.shape["tile"], mesh.shape["slab"]),
        mesh=mesh,
        in_specs=placed,
        out_specs=P(("clip", "slab"), "tile", None, "chan"),
        check_vma=False,
    )
```

```python
import functools

import jax
import jax.numpy as jnp
from jax import lax
from jax.experimental import pallas as pl
from jax.experimental.pallas import tpu as pltpu
from jax.sharding import PartitionSpec as P

MESH = pl.DeviceIdType.MESH
BACK = 2


def kernel(
    tiles, slabs, video, w1, b1, w2, b2, out,
    v, h, k1, k2, bias1, bias2, pieces, incoming, going, going0, sum0, acc, acc2,
    load, w_s, b_s, z0_s, w1_r, b_r, a_r, z_r, f_r, q_r, o_r,
):
    x_s, p_s, o_s, q_s, z1_s = (load.at[n] for n in range(5))
    z_s = (z0_s, z1_s)
    frames, rows, columns, channels = video.shape
    half = rows // 2
    width = b2.shape[1]
    core = lax.axis_index("chan")
    tile = lax.axis_index("tile")
    slab = lax.axis_index("slab")
    other = 1 - core
    z_tile = tile + 2 * core - 1
    has_z = jnp.logical_and(z_tile >= 0, z_tile < tiles)
    no_z = jnp.logical_or(z_tile < 0, z_tile >= tiles)
    has_next = slab < slabs - 1
    no_next = slab == slabs - 1
    has_prev = slab > 0
    no_prev = slab == 0
    one = core == 1
    zero = core == 0
    above = tile > 0
    below = tile < tiles - 1
    peer = {"chan": other}
    z_minus = {"tile": tile - 1, "chan": 1}
    z_plus = {"tile": tile + 1, "chan": 0}
    next_same = {"slab": slab + 1}
    next_cross = {"slab": slab + 1, "chan": other}
    prev_same = {"slab": slab - 1}

    def both(*conditions):
        return functools.reduce(jnp.logical_and, conditions)

    def when(condition, body):
        if condition is None:
            body()
        else:
            pl.when(condition)(body)

    barrier = pltpu.get_barrier_semaphore()
    greetings = (
        (None, peer),
        (has_z, {"chan": other, "tile": z_tile}),
        (has_prev, {"slab": slab - 1, "chan": 1}),
    )
    for condition, device in greetings:
        when(condition, lambda device=device: pl.semaphore_signal(
            barrier, inc=1, device_id=device, device_id_type=MESH))
    met = 1
    for condition, count in ((has_z, 1), (both(one, has_next), 2)):
        met = met + jnp.where(condition, count, 0)

    into_v = pltpu.make_async_copy(video, v.at[pl.ds(BACK, frames), pl.ds(half * other, rows)], load.at[0])
    own_w1 = pltpu.make_async_copy(w1, k1.at[:, :, core], load.at[1])
    own_b1 = pltpu.make_async_copy(b1, bias1.at[core], load.at[2])
    own_b2 = pltpu.make_async_copy(b2, bias2.at[0], load.at[4])
    own_w2 = [
        pltpu.make_async_copy(
            w2.at[:, :, :, pl.ds(pl.multiple_of(owner * width, width), width)], k2.at[n], load.at[3])
        for n, owner in enumerate((core, other))
    ]
    for copy in (into_v, own_w1, own_b1, own_b2):
        copy.start()

    def remote(src, dst, send, recv, device):
        return pltpu.make_async_remote_copy(
            src_ref=src, dst_ref=dst, send_sem=send, recv_sem=recv,
            device_id=device, device_id_type=MESH,
        )

    def wait_bytes(ref, semaphore):
        pltpu.make_async_copy(ref, ref, semaphore).wait()

    mine = pl.ds(half * core, half)
    theirs = pl.ds(half * other, half)
    halo_here = pl.ds(rows * core, half)
    frame0, frame1 = frames, frames + 1

    low, high = pl.ds(0, half), pl.ds(half, half)
    halo_low, halo_high = pl.ds(0, half), pl.ds(rows, half)

    def x_copies(device):
        return [
            [
                remote(v.at[frames + f, some], v.at[f, some], x_s, a_r.at[2 * f + n], device)
                for n, some in enumerate((low, high))
            ]
            for f in range(BACK)
        ]

    x_out = x_copies(next_same)
    x_in = x_copies(prev_same)
    forward_z = [
        [
            (above, remote(v.at[f, low], v.at[f, halo_high], z_s[0], f_r.at[f], z_minus)),
            (below, remote(v.at[f, high], v.at[f, halo_low], z_s[1], f_r.at[f], z_plus)),
        ]
        for f in range(BACK)
    ]
    f_in = [remote(v.at[f, low], v.at[f, halo_low], z_s[0], f_r.at[f], peer) for f in range(BACK)]
    forward_p = [remote(v.at[f, low], v.at[f, pl.ds(half, half)], p_s, a_r.at[f], peer) for f in range(BACK)]

    def share_h(index, count, place):
        return remote(
            h.at[pl.ds(index, count), low], h.at[pl.ds(index, count), pl.ds(half, half)], p_s, a_r.at[2 + place], peer
        )

    forward_h = [share_h(BACK, 1, 0), share_h(BACK + 1, 1, 1), share_h(frames, 2, 2), share_h(frames, 1, 2)]

    rest_h = [
        remote(
            h.at[pl.ds(BACK + n, n + 1), high], h.at[pl.ds(BACK + n, n + 1), pl.ds(rows, half)], o_s, a_r.at[n], peer
        )
        for n in range(2)
    ]

    def z_copies(count):
        some = pl.ds(BACK, count)
        return [
            [
                remote(video.at[pl.ds(0, count), pl.ds(n, 1)], v.at[some, pl.ds(rows + n, 1)], z_s[0], z_r.at[n], z_minus)
                for n in range(half)
            ],
            [
                remote(
                    v.at[some, pl.ds(rows - 1 - n, 1)], v.at[some, pl.ds(half - 1 - n, 1)], z_s[1], z_r.at[n], z_plus
                )
                for n in range(half)
            ],
        ]

    z_full = z_copies(frames)
    z_short = z_copies(frames - 1)

    def start_z(side):
        for condition, copies in ((has_next, z_full), (no_next, z_short)):

            @pl.when(condition)
            def _():
                for copy in copies[side]:
                    copy.start()

    to_peer = [
        remote(w1, k1.at[:, :, core], w_s, w1_r, peer),
        remote(b1, bias1.at[core], b_s.at[0], b_r.at[0], peer),
        remote(b2, bias2.at[1], b_s.at[1], b_r.at[1], peer),
    ]

    with jax.named_scope("entrybar"):
        pl.semaphore_wait(barrier, met)

    @pl.when(both(zero, above))
    def _():
        start_z(0)

    for copy in to_peer:
        copy.start()
    with jax.named_scope("loadwait"):
        into_v.wait()
        own_w1.wait()
        own_b1.wait()
        own_b2.wait()

    @pl.when(one)
    def _():
        @pl.when(has_next)
        def _():
            for f in (1, 0):
                for n in range(2):
                    x_out[f][n].start()

        @pl.when(below)
        def _():
            start_z(1)

    for copy in own_w2:
        copy.start()

    @pl.when(no_z)
    def _():
        v[:, halo_here] = jnp.zeros((v.shape[0], half, columns, channels), v.dtype)

    def taps(source, index, first, count, steps):
        return jnp.concatenate(
            [
                source[index + a, pl.ds(first + b, count)].reshape(count * columns, channels)
                for a in steps
                for b in range(3)
            ],
            axis=1,
        )

    def shifted(parts, size):
        column = lax.broadcasted_iota(jnp.int32, (parts.shape[0], size), 0) % columns
        before = pltpu.roll(parts[:, 0:size], 1, 0)
        after = pltpu.roll(parts[:, 2 * size : 3 * size], parts.shape[0] - 1, 0)
        total = parts[:, size : 2 * size] + jnp.where(column == 0, 0.0, before)
        return total + jnp.where(column == columns - 1, 0.0, after)

    def silu(total):
        return total / (1.0 + jnp.exp(-total))

    def hidden_sum(indices, first, count, steps):
        parts = lax.dot_general(
            jnp.concatenate([taps(v, index - 2, first, count, steps) for index in indices], axis=0),
            jnp.concatenate(
                [k1[3 * a + b].reshape(3 * channels, channels) for a in steps for b in range(3)], axis=1
            ),
            (((1,), (1,)), ((), ())),
            preferred_element_type=jnp.float32,
        )
        return shifted(parts, channels)

    def hidden(indices, first, count, oldest=0, newest=2, before=None):
        total = hidden_sum(indices, first, count, range(oldest, newest + 1))
        if before is not None:
            total = total + before
        bias = jnp.concatenate([bias1[0], bias1[1]], axis=1)
        value = silu(total + bias).astype(h.dtype)
        value = value.reshape(len(indices), count, columns, channels)
        for n, index in enumerate(indices):
            h[index, pl.ds(first, count)] = value[n]

    def inner(*indices, oldest=0):
        with jax.named_scope("inner" + "_".join(map(str, indices))):
            hidden(indices, half * other, half, oldest)

    def clear_outside(index):
        @pl.when(no_z)
        def _():
            h[index, pl.ds((rows - 1) * core, 1)] = jnp.zeros((1, columns, channels), h.dtype)

    def outer(*indices, oldest=0):
        with jax.named_scope("outer" + "_".join(map(str, indices))):
            hidden(indices, half * core, half, oldest)
            for index in indices:
                clear_outside(index)

    def near(*indices, oldest=0):
        with jax.named_scope("near" + "_".join(map(str, indices))):
            hidden(indices, 1 + core, 1, oldest)

    def far(*indices, oldest=0):
        with jax.named_scope("far" + "_".join(map(str, indices))):

            @pl.when(has_z)
            def _():
                hidden(indices, (rows - 1) * core, 1, oldest)

            for index in indices:
                clear_outside(index)

    def outer_begin(index):
        with jax.named_scope("outer%da" % index):
            acc2[...] = hidden_sum((index,), half * core, half, range(1, 3))

    def outer_end(index):
        with jax.named_scope("outer%db" % index):
            hidden((index,), half * core, half, 0, 0, acc2[...])
            clear_outside(index)

    def second(index, first, count, steps, blocks):
        matrix = jnp.concatenate(
            [
                jnp.concatenate([k2[n, 3 * (a + shift) + b, e] for n, shift in blocks for e in range(3)], axis=1)
                for a in steps
                for b in range(3)
            ],
            axis=0,
        )
        parts = jnp.dot(taps(h, index, first, count, steps), matrix, preferred_element_type=jnp.float32)
        return [shifted(parts[:, 3 * k * width : 3 * (k + 1) * width], width) for k in range(len(blocks))]

    whole = ((0, 0), (1, 0))

    def share(slot, local):
        place = half * core + local
        return [
            remote(pieces.at[slot, 0], incoming.at[place], q_s, q_r.at[slot], next_same),
            remote(pieces.at[slot, 1], incoming.at[place], q_s, q_r.at[slot], next_cross),
        ]

    shares = [share(0, other), share(1, core)]

    def send_share(slot, local):
        with jax.named_scope("share%d" % slot):
            halves = second(frames, local, 1, range(0, 2), whole)
            for n in (1, 0):
                pieces[slot, n] = halves[n].astype(pieces.dtype)
                shares[slot][n].start()

    result = [
        remote(going.at[t - 1], out.at[t, mine], o_s, o_r.at[t], peer) for t in range(1, frames // 2)
    ]
    part0 = remote(going0, sum0.at[mine], o_s, o_r.at[0], peer)

    def latent(t):
        with jax.named_scope("latent%d" % t):
            own, away = second(2 * t, 0, half, range(3), whole)
            going[t - 1] = silu(away + bias2[1]).astype(out.dtype).reshape(half, columns, width)
            result[t - 1].start()
            out[t, mine] = silu(own + bias2[0]).astype(out.dtype).reshape(half, columns, width)

    def later_steps(steps=range(1, 3), start=True):
        with jax.named_scope("latent1a%d" % len(steps)):
            halves = second(2, 0, half, steps, whole)
            for n in range(2):
                acc[n] = halves[n] if start else acc[n] + halves[n]

    def own_steps(first, ready=None):
        place = pl.ds(half * core if first == 0 else half, half)
        with jax.named_scope("own1a"):
            acc[0] = second(2, first, half, range(1, 3), ((0, 0),))[0]
        if ready is not None:
            ready()
        with jax.named_scope("own"):
            one_sum, then = second(2, first, half, range(0, 1), ((0, 2), (0, 0)))
            sum0[place] = one_sum.reshape(half, columns, width)
            out[1, place] = silu(then + acc[0] + bias2[0]).astype(out.dtype).reshape(half, columns, width)

    def last_steps():
        with jax.named_scope("tailA"):
            first, then = second(2, 0, half, range(0, 1), ((1, 2), (1, 0)))
            going0[...] = first.reshape(half, columns, width)
            part0.start()
            going[0] = silu(then + acc[1] + bias2[1]).astype(out.dtype).reshape(half, columns, width)
            result[0].start()
        with jax.named_scope("tailB"):
            first, then = second(2, 0, half, range(0, 1), ((0, 2), (0, 0)))
            sum0[mine] = first.reshape(half, columns, width)
            out[1, mine] = silu(then + acc[0] + bias2[0]).astype(out.dtype).reshape(half, columns, width)

    def wait_z(which, copies):
        with jax.named_scope("zwait%d" % which):

            @pl.when(has_z)
            def _():
                copies[0][which].wait_recv()

    def pass_on(f, n):
        with jax.named_scope("pass%d%d" % (f, n)):
            x_in[f][n].wait_recv()
            condition, copy = forward_z[f][n]
            pl.when(condition)(copy.start)
            if n == 0:
                forward_p[f].start()

    def from_peer(name, copy):
        @pl.when(zero)
        def _():
            with jax.named_scope(name):
                copy.wait_recv()

    def halo_ready(name, copy):
        with jax.named_scope(name):

            @pl.when(has_z)
            def _():
                copy.wait_recv()

    def w2_ready():
        with jax.named_scope("w2wait"):
            wait_bytes(k2, load.at[3])

    with jax.named_scope("w1wait"):
        remote(w1, k1.at[:, :, other], w_s, w1_r, peer).wait_recv()
        remote(b1, bias1.at[other], b_s.at[0], b_r.at[0], peer).wait_recv()
        to_peer[2].wait_recv()

    last = frames + 1

    @pl.when(both(one, has_next))
    def _():
        inner(frames, last)
        forward_h[2].start()

    @pl.when(both(one, no_next))
    def _():
        inner(frames)
        forward_h[3].start()

    @pl.when(both(one, no_prev))
    def _():
        inner(3, oldest=1)
        forward_h[1].start()
        inner(2, oldest=2)
        forward_h[0].start()

    @pl.when(has_next)
    def _():
        wait_z(0, z_full)
        near(frames, last)
        w2_ready()
        from_peer("hwait2", forward_h[2])
        send_share(0, other)

        wait_z(1, z_full)
        far(frames, last)

        @pl.when(has_prev)
        def _():
            send_share(1, core)

    def middle():
        for index in range(frames - 1, 3, -1):
            inner(index)
            outer(index)
        for t in range(2, frames // 2):
            latent(t)

    def own_last():
        @pl.when(no_next)
        def _():
            wait_z(0, z_short)
            wait_z(1, z_short)
            outer(frames)

    def own_ready():
        @pl.when(no_next)
        def _():
            w2_ready()
            from_peer("hwait2", forward_h[3])

    @pl.when(no_prev)
    def _():
        own_last()
        own_ready()
        middle()

        outer(3, oldest=1)

        @pl.when(one)
        def _():
            rest_h[1].start()

        @pl.when(has_next)
        def _():
            send_share(1, core)

        outer(2, oldest=2)

        @pl.when(one)
        def _():
            rest_h[0].start()

        @pl.when(one)
        def _():
            own_steps(0)

        @pl.when(zero)
        def _():
            forward_h[1].wait_recv()
            later_steps()
            forward_h[0].wait_recv()
            last_steps()
            with jax.named_scope("rest"):
                rest_h[1].wait_recv()
            own_steps(half, rest_h[0].wait_recv)

    @pl.when(has_prev)
    def _():
        @pl.when(one)
        def _():
            pass_on(1, 0)
            pass_on(1, 1)
            inner(3)
            forward_h[1].start()
            pass_on(0, 0)
            own_last()
            pass_on(0, 1)
            inner(2)
            forward_h[0].start()

        @pl.when(zero)
        def _():
            own_last()

        own_ready()
        middle()
        later_steps(range(2, 3))
        from_peer("pwait1", forward_p[1])
        halo_ready("fwait1", f_in[1])
        outer(3)
        from_peer("hwait1", forward_h[1])
        later_steps(range(1, 2), False)
        outer_begin(2)
        from_peer("pwait0", forward_p[0])
        halo_ready("fwait0", f_in[0])
        outer_end(2)
        from_peer("hwait0", forward_h[0])
        last_steps()


    takes = jnp.logical_or(has_prev, one)

    @pl.when(takes)
    def _():
        remote(going0, sum0.at[theirs], o_s, o_r.at[0], peer).wait_recv()

    def close(first, count, extra):
        total = sum0[pl.ds(first, count)].reshape(count * columns, width)
        if extra:
            total = total + incoming[pl.ds(first, count)].reshape(count * columns, width).astype(jnp.float32)
        out[0, pl.ds(first, count)] = silu(total + bias2[0]).astype(out.dtype).reshape(count, columns, width)

    @pl.when(has_prev)
    def _():
        for slot, pair in enumerate(((half - 1, half), (0, rows - 1))):
            with jax.named_scope("close%d" % slot):
                wait_bytes(pieces.at[0], q_r.at[slot])
                for row in pair:
                    close(row, 1, True)

    @pl.when(no_prev)
    def _():
        close(0, rows, False)

    with jax.named_scope("ends"):
        for copy in to_peer:
            copy.wait_send()
        for t in range(1, frames // 2):
            copy = remote(going.at[t - 1], out.at[t, theirs], o_s, o_r.at[t], peer)
            when(takes if t == 1 else None, copy.wait_recv)
        wait_bytes(v.at[pl.ds(0, frames // 2 + 1), low], o_s)

        @pl.when(has_next)
        def _():
            wait_bytes(incoming, q_s)

        @pl.when(both(one, has_next))
        def _():
            wait_bytes(v.at[pl.ds(0, BACK), pl.ds(0, rows)], x_s)

        for condition, count in (
            (both(no_prev, has_next), 4), (both(no_prev, no_next), 3),
            (both(has_prev, has_next), 6), (both(has_prev, no_next), 5),
        ):

            @pl.when(both(one, condition))
            def _():
                wait_bytes(v.at[pl.ds(0, count), low], p_s)

        for side, condition in ((0, above), (1, below)):
            forwards = both(one, condition)
            for after, count in ((has_next, frames), (no_next, frames - 1)):
                if side == 0:

                    @pl.when(both(zero, condition, after))
                    def _():
                        wait_bytes(v.at[pl.ds(0, count), low], z_s[0])

                else:

                    @pl.when(both(forwards, after, no_prev))
                    def _():
                        wait_bytes(v.at[pl.ds(0, count), low], z_s[1])

                    @pl.when(both(forwards, after, has_prev))
                    def _():
                        wait_bytes(v.at[pl.ds(0, count + BACK), low], z_s[1])

            if side == 0:

                @pl.when(both(forwards, has_prev))
                def _():
                    wait_bytes(v.at[pl.ds(0, BACK), low], z_s[0])


def shards(tiles, slabs, video, first_weight, first_bias, second_weight, second_bias):
    frames, rows, columns, channels = video.shape
    half = rows // 2
    assert half == 2 and first_weight.shape[3] == channels == second_bias.shape[0] and frames >= 4 and frames % 2 == 0
    part = first_bias.shape[0]
    width = second_bias.shape[0]
    anywhere = pl.BlockSpec(memory_space=pltpu.HBM)
    inside = pl.BlockSpec(memory_space=pltpu.VMEM)
    dma = pltpu.SemaphoreType.DMA
    vmem = pltpu.VMEM
    latents = frames // 2
    return pl.pallas_call(
        functools.partial(kernel, tiles, slabs),
        out_shape=jax.ShapeDtypeStruct((latents, rows, columns, width), jnp.bfloat16),
        in_specs=[anywhere] * 5,
        out_specs=inside,
        scratch_shapes=[
            vmem((BACK + frames, rows + 2, columns, channels), jnp.bfloat16),
            vmem((frames + 2, half + 4, columns, channels), jnp.bfloat16),
            vmem((9, 3, 2, part, channels), jnp.bfloat16),
            vmem((2, 9, 3, channels, width), jnp.bfloat16),
            vmem((2, 1, part), jnp.float32),
            vmem((2, 1, width), jnp.float32),
            vmem((2, 2, columns, width), jnp.bfloat16),
            vmem((rows, columns, width), jnp.bfloat16),
            vmem((latents - 1, half, columns, width), jnp.bfloat16),
            vmem((half, columns, width), jnp.float32),
            vmem((rows, columns, width), jnp.float32),
            vmem((2, half * columns, width), jnp.float32),
            vmem((half * columns, channels), jnp.float32),
            dma((5,)), dma, dma((2,)), dma, dma, dma((2,)), dma((2 * BACK + 1,)), dma((2,)), dma((BACK,)), dma((2,)),
            dma((latents,)),
        ],
        compiler_params=pltpu.CompilerParams(
            collective_id=0, has_side_effects=True, vmem_limit_bytes=32 << 20
        ),
    )(
        *(
            pltpu.with_memory_space_constraint(operand, pltpu.HBM)
            for operand in (
                video,
                jnp.swapaxes(first_weight, 3, 4).reshape(9, 3, part, channels),
                first_bias.reshape(1, part),
                second_weight.reshape(9, 3, channels, 2 * width),
                second_bias.reshape(1, width),
            )
        )
    )


def solution(mesh):
    placed = (
        P(("clip", "slab"), "tile", None, None),
        P(None, None, None, None, "chan"),
        P("chan"),
        P(),
        P("chan"),
    )
    return jax.shard_map(
        functools.partial(shards, mesh.shape["tile"], mesh.shape["slab"]),
        mesh=mesh,
        in_specs=placed,
        out_specs=P(("clip", "slab"), "tile", None, "chan"),
        check_vma=False,
    )
```

```python
import functools

import jax
import jax.numpy as jnp
from jax import lax
from jax.experimental import pallas as pl
from jax.experimental.pallas import tpu as pltpu
from jax.sharding import PartitionSpec as P

MESH = pl.DeviceIdType.MESH
BACK = 2


def kernel(
    tiles, slabs, video, w1, b1, w2, b2, out,
    v, h, k1, k2, bias1, bias2, pieces, incoming, going, going0, sum0, acc, acc2,
    load, w_s, b_s, z0_s, w1_r, b_r, a_r, z_r, f_r, q_r, o_r,
):
    x_s, p_s, o_s, q_s, z1_s = (load.at[n] for n in range(5))
    z_s = (z0_s, z1_s)
    frames, rows, columns, channels = video.shape
    half = rows // 2
    width = b2.shape[1]
    core = lax.axis_index("chan")
    tile = lax.axis_index("tile")
    slab = lax.axis_index("slab")
    other = 1 - core
    z_tile = tile + 2 * core - 1
    has_z = jnp.logical_and(z_tile >= 0, z_tile < tiles)
    no_z = jnp.logical_or(z_tile < 0, z_tile >= tiles)
    has_next = slab < slabs - 1
    no_next = slab == slabs - 1
    has_prev = slab > 0
    no_prev = slab == 0
    one = core == 1
    zero = core == 0
    above = tile > 0
    below = tile < tiles - 1
    peer = {"chan": other}
    z_minus = {"tile": tile - 1, "chan": 1}
    z_plus = {"tile": tile + 1, "chan": 0}
    next_same = {"slab": slab + 1}
    next_cross = {"slab": slab + 1, "chan": other}
    prev_same = {"slab": slab - 1}

    def both(*conditions):
        return functools.reduce(jnp.logical_and, conditions)

    def when(condition, body):
        if condition is None:
            body()
        else:
            pl.when(condition)(body)

    barrier = pltpu.get_barrier_semaphore()
    greetings = (
        (None, peer),
        (has_z, {"chan": other, "tile": z_tile}),
        (has_prev, {"slab": slab - 1, "chan": 1}),
        (both(one, has_prev, below), {"slab": slab - 1, "tile": tile + 1, "chan": 1}),
    )
    for condition, device in greetings:
        when(condition, lambda device=device: pl.semaphore_signal(
            barrier, inc=1, device_id=device, device_id_type=MESH))
    met = 1
    for condition, count in ((has_z, 1), (both(one, has_next), 2), (both(one, has_next, above), 1)):
        met = met + jnp.where(condition, count, 0)

    into_v = pltpu.make_async_copy(video, v.at[pl.ds(BACK, frames), pl.ds(half * other, rows)], load.at[0])
    own_w1 = pltpu.make_async_copy(w1, k1.at[:, :, core], load.at[1])
    own_b1 = pltpu.make_async_copy(b1, bias1.at[core], load.at[2])
    own_b2 = pltpu.make_async_copy(b2, bias2.at[0], load.at[4])
    own_w2 = [
        pltpu.make_async_copy(
            w2.at[:, :, :, pl.ds(pl.multiple_of(owner * width, width), width)], k2.at[n], load.at[3])
        for n, owner in enumerate((core, other))
    ]
    for copy in (into_v, own_w1, own_b1, own_b2):
        copy.start()

    def remote(src, dst, send, recv, device):
        return pltpu.make_async_remote_copy(
            src_ref=src, dst_ref=dst, send_sem=send, recv_sem=recv,
            device_id=device, device_id_type=MESH,
        )

    def wait_bytes(ref, semaphore):
        pltpu.make_async_copy(ref, ref, semaphore).wait()

    mine = pl.ds(half * core, half)
    theirs = pl.ds(half * other, half)
    halo_here = pl.ds(rows * core, half)
    frame0, frame1 = frames, frames + 1

    low, high = pl.ds(0, half), pl.ds(half, half)
    halo_low, halo_high = pl.ds(0, half), pl.ds(rows, half)

    def x_copies(device):
        return [
            [
                remote(v.at[frames + f, some], v.at[f, some], x_s, a_r.at[2 * f + n], device)
                for n, some in enumerate((low, high))
            ]
            for f in range(BACK)
        ]

    x_out = x_copies(next_same)
    x_in = x_copies(prev_same)
    slanted = remote(v.at[frames, low], v.at[0, halo_high], x_s, f_r.at[0], {"slab": slab + 1, **z_minus})
    forward_z = [
        [
            (above, remote(v.at[f, low], v.at[f, halo_high], z_s[0], f_r.at[f], z_minus)),
            (below, remote(v.at[f, high], v.at[f, halo_low], z_s[1], f_r.at[f], z_plus)),
        ]
        for f in range(BACK)
    ]
    f_in = [remote(v.at[f, low], v.at[f, halo_low], z_s[0], f_r.at[f], peer) for f in range(BACK)]
    forward_p = [remote(v.at[f, low], v.at[f, pl.ds(half, half)], p_s, a_r.at[f], peer) for f in range(BACK)]

    def share_h(index, count, place):
        return remote(
            h.at[pl.ds(index, count), low], h.at[pl.ds(index, count), pl.ds(half, half)], p_s, a_r.at[2 + place], peer
        )

    forward_h = [share_h(BACK, 1, 0), share_h(BACK + 1, 1, 1), share_h(frames, 2, 2), share_h(frames, 1, 2)]

    rest_h = [
        remote(
            h.at[pl.ds(BACK + n, n + 1), high], h.at[pl.ds(BACK + n, n + 1), pl.ds(rows, half)], o_s, a_r.at[n], peer
        )
        for n in range(2)
    ]

    def z_copies(count):
        some = pl.ds(BACK, count)
        return [
            [
                remote(video.at[pl.ds(0, count), pl.ds(n, 1)], v.at[some, pl.ds(rows + n, 1)], z_s[0], z_r.at[n], z_minus)
                for n in range(half)
            ],
            [
                remote(
                    v.at[some, pl.ds(rows - 1 - n, 1)], v.at[some, pl.ds(half - 1 - n, 1)], z_s[1], z_r.at[n], z_plus
                )
                for n in range(half)
            ],
        ]

    z_full = z_copies(frames)
    z_short = z_copies(frames - 1)

    def start_z(side):
        for condition, copies in ((has_next, z_full), (no_next, z_short)):

            @pl.when(condition)
            def _():
                for copy in copies[side]:
                    copy.start()

    to_peer = [
        remote(w1, k1.at[:, :, core], w_s, w1_r, peer),
        remote(b1, bias1.at[core], b_s.at[0], b_r.at[0], peer),
        remote(b2, bias2.at[1], b_s.at[1], b_r.at[1], peer),
    ]

    with jax.named_scope("entrybar"):
        pl.semaphore_wait(barrier, met)

    @pl.when(both(zero, above))
    def _():
        start_z(0)

    for copy in to_peer:
        copy.start()
    with jax.named_scope("loadwait"):
        into_v.wait()
        own_w1.wait()
        own_b1.wait()
        own_b2.wait()

    @pl.when(one)
    def _():
        @pl.when(has_next)
        def _():
            for f in (1, 0):
                for n in range(2):
                    x_out[f][n].start()

        @pl.when(below)
        def _():
            start_z(1)

    for copy in own_w2:
        copy.start()

    @pl.when(no_z)
    def _():
        v[:, halo_here] = jnp.zeros((v.shape[0], half, columns, channels), v.dtype)

    def taps(source, index, first, count, steps):
        return jnp.concatenate(
            [
                source[index + a, pl.ds(first + b, count)].reshape(count * columns, channels)
                for a in steps
                for b in range(3)
            ],
            axis=1,
        )

    def shifted(parts, size):
        column = lax.broadcasted_iota(jnp.int32, (parts.shape[0], size), 0) % columns
        before = pltpu.roll(parts[:, 0:size], 1, 0)
        after = pltpu.roll(parts[:, 2 * size : 3 * size], parts.shape[0] - 1, 0)
        total = parts[:, size : 2 * size] + jnp.where(column == 0, 0.0, before)
        return total + jnp.where(column == columns - 1, 0.0, after)

    def silu(total):
        return total / (1.0 + jnp.exp(-total))

    def hidden_sum(indices, first, count, steps):
        parts = lax.dot_general(
            jnp.concatenate([taps(v, index - 2, first, count, steps) for index in indices], axis=0),
            jnp.concatenate(
                [k1[3 * a + b].reshape(3 * channels, channels) for a in steps for b in range(3)], axis=1
            ),
            (((1,), (1,)), ((), ())),
            preferred_element_type=jnp.float32,
        )
        return shifted(parts, channels)

    no_rows = {"inner": (), "near": (), "far": (no_z,), "outer": (both(no_z, zero), both(no_z, one))}

    def hidden(kind, indices, first, count, oldest=0, newest=2, before=None):
        total = hidden_sum(indices, first, count, range(oldest, newest + 1))
        if before is not None:
            total = total + before
        bias = jnp.concatenate([bias1[0], bias1[1]], axis=1)
        value = silu(total + bias)
        value = value.reshape(len(indices), count, columns, channels)
        for n, index in enumerate(indices):
            new = value[n]
            if no_rows[kind]:
                new = jnp.stack([jnp.where(no_rows[kind][row], 0.0, new[row]) for row in range(count)])
            h[index, pl.ds(first, count)] = new.astype(h.dtype)

    def inner(*indices, oldest=0):
        with jax.named_scope("inner" + "_".join(map(str, indices))):
            hidden("inner", indices, half * other, half, oldest)

    def outer(*indices, oldest=0):
        with jax.named_scope("outer" + "_".join(map(str, indices))):
            hidden("outer", indices, half * core, half, oldest)

    def near(*indices, oldest=0):
        with jax.named_scope("near" + "_".join(map(str, indices))):
            hidden("near", indices, 1 + core, 1, oldest)

    def far(*indices, oldest=0):
        with jax.named_scope("far" + "_".join(map(str, indices))):
            hidden("far", indices, (rows - 1) * core, 1, oldest)

    def outer_begin(index):
        with jax.named_scope("outer%da" % index):
            acc2[...] = hidden_sum((index,), half * core, half, range(1, 3))

    def outer_end(index):
        with jax.named_scope("outer%db" % index):
            hidden("outer", (index,), half * core, half, 0, 0, acc2[...])

    def second(index, first, count, steps, blocks):
        matrix = jnp.concatenate(
            [
                jnp.concatenate([k2[n, 3 * (a + shift) + b, e] for n, shift in blocks for e in range(3)], axis=1)
                for a in steps
                for b in range(3)
            ],
            axis=0,
        )
        parts = jnp.dot(taps(h, index, first, count, steps), matrix, preferred_element_type=jnp.float32)
        return [shifted(parts[:, 3 * k * width : 3 * (k + 1) * width], width) for k in range(len(blocks))]

    whole = ((0, 0), (1, 0))

    def share(slot, local):
        place = half * core + local
        return [
            remote(pieces.at[slot, 0], incoming.at[place], q_s, q_r.at[slot], next_same),
            remote(pieces.at[slot, 1], incoming.at[place], q_s, q_r.at[slot], next_cross),
        ]

    shares = [share(0, other), share(1, core)]

    def send_share(slot, local):
        with jax.named_scope("share%d" % slot):
            halves = second(frames, local, 1, range(0, 2), whole)
            for n in (1, 0):
                pieces[slot, n] = halves[n].astype(pieces.dtype)
                shares[slot][n].start()

    result = [
        remote(going.at[t - 1], out.at[t, mine], o_s, o_r.at[t], peer) for t in range(1, frames // 2)
    ]
    part0 = remote(going0, sum0.at[mine], o_s, o_r.at[0], peer)

    def latent(t):
        with jax.named_scope("latent%d" % t):
            own, away = second(2 * t, 0, half, range(3), whole)
            going[t - 1] = silu(away + bias2[1]).astype(out.dtype).reshape(half, columns, width)
            result[t - 1].start()
            out[t, mine] = silu(own + bias2[0]).astype(out.dtype).reshape(half, columns, width)

    def later_steps(steps=range(1, 3), start=True):
        with jax.named_scope("latent1a%d" % len(steps)):
            halves = second(2, 0, half, steps, whole)
            for n in range(2):
                acc[n] = halves[n] if start else acc[n] + halves[n]

    def own_steps(first, ready=lambda: None):
        place = pl.ds(half * core if first == 0 else half, half)
        with jax.named_scope("own1a"):
            acc[0] = second(2, first, half, range(1, 3), ((0, 0),))[0]
        ready()
        with jax.named_scope("own"):
            one_sum, then = second(2, first, half, range(0, 1), ((0, 2), (0, 0)))
            sum0[place] = one_sum.reshape(half, columns, width)
            out[1, place] = silu(then + acc[0] + bias2[0]).astype(out.dtype).reshape(half, columns, width)

    def last_steps():
        with jax.named_scope("tailA"):
            first, then = second(2, 0, half, range(0, 1), ((1, 2), (1, 0)))
            going0[...] = first.reshape(half, columns, width)
            part0.start()
            going[0] = silu(then + acc[1] + bias2[1]).astype(out.dtype).reshape(half, columns, width)
            result[0].start()
        with jax.named_scope("tailB"):
            first, then = second(2, 0, half, range(0, 1), ((0, 2), (0, 0)))
            sum0[mine] = first.reshape(half, columns, width)
            out[1, mine] = silu(then + acc[0] + bias2[0]).astype(out.dtype).reshape(half, columns, width)

    def wait_z(which, copies):
        with jax.named_scope("zwait%d" % which):

            @pl.when(has_z)
            def _():
                copies[0][which].wait_recv()

    def pass_on(f, n):
        with jax.named_scope("pass%d%d" % (f, n)):
            x_in[f][n].wait_recv()
            condition, copy = forward_z[f][n]
            if (f, n) != (0, 0):
                pl.when(condition)(copy.start)
            if n == 0:
                forward_p[f].start()

    def from_peer(name, copy):
        @pl.when(zero)
        def _():
            with jax.named_scope(name):
                copy.wait_recv()

    def halo_ready(name, copy):
        with jax.named_scope(name):

            @pl.when(has_z)
            def _():
                copy.wait_recv()

    def w2_ready():
        with jax.named_scope("w2wait"):
            wait_bytes(k2, load.at[3])

    with jax.named_scope("w1wait"):
        remote(w1, k1.at[:, :, other], w_s, w1_r, peer).wait_recv()
        remote(b1, bias1.at[other], b_s.at[0], b_r.at[0], peer).wait_recv()
        to_peer[2].wait_recv()

    last = frames + 1

    @pl.when(both(one, has_next))
    def _():
        inner(frames, last)
        forward_h[2].start()

    @pl.when(both(one, no_next))
    def _():
        inner(frames)
        forward_h[3].start()

    @pl.when(both(one, no_prev))
    def _():
        inner(3, oldest=1)
        forward_h[1].start()
        inner(2, oldest=2)
        forward_h[0].start()

    @pl.when(both(one, has_next, above))
    def _():
        slanted.start()

    @pl.when(has_next)
    def _():
        wait_z(0, z_full)
        near(frames, last)
        w2_ready()
        from_peer("hwait2", forward_h[2])
        send_share(0, other)

        wait_z(1, z_full)

        @pl.when(jnp.logical_or(above, has_prev))
        def _():
            far(frames, last)
            send_share(1, core)

    def middle():
        for index in range(frames - 1, 3, -1):
            inner(index)
            outer(index)
        for t in range(2, frames // 2):
            latent(t)

    def own_last():
        @pl.when(no_next)
        def _():
            wait_z(0, z_short)
            wait_z(1, z_short)
            outer(frames)

    def own_ready():
        @pl.when(no_next)
        def _():
            w2_ready()
            from_peer("hwait2", forward_h[3])

    @pl.when(no_prev)
    def _():
        own_last()
        own_ready()
        middle()

        @pl.when(both(has_next, tile == 0))
        def _():
            far(frames, last)
            outer(3, oldest=1)
            outer(2, oldest=2)

        @pl.when(jnp.logical_or(above, no_next))
        def _():
            outer(3, oldest=1)
            outer(2, oldest=2)

        @pl.when(one)
        def _():
            rest_h[1].start()
            rest_h[0].start()

        @pl.when(both(has_next, tile == 0))
        def _():
            send_share(1, core)

        @pl.when(one)
        def _():
            own_steps(0)

        @pl.when(zero)
        def _():
            forward_h[1].wait_recv()
            forward_h[0].wait_recv()
            later_steps()
            last_steps()
            rest_h[1].wait_recv()
            own_steps(half, rest_h[0].wait_recv)

    @pl.when(has_prev)
    def _():
        @pl.when(one)
        def _():
            pass_on(1, 0)
            pass_on(1, 1)
            inner(3)
            forward_h[1].start()
            pass_on(0, 0)
            own_last()
            pass_on(0, 1)
            inner(2)
            forward_h[0].start()

        @pl.when(zero)
        def _():
            own_last()

        own_ready()
        middle()
        later_steps(range(2, 3))
        from_peer("pwait1", forward_p[1])
        halo_ready("fwait1", f_in[1])
        from_peer("hwait1", forward_h[1])
        outer(3)
        later_steps(range(1, 2), False)
        outer_begin(2)
        from_peer("pwait0", forward_p[0])
        from_peer("hwait0", forward_h[0])
        halo_ready("fwait0", f_in[0])
        outer_end(2)
        last_steps()


    takes = jnp.logical_or(has_prev, one)

    @pl.when(takes)
    def _():
        remote(going0, sum0.at[theirs], o_s, o_r.at[0], peer).wait_recv()

    def close(first, count, extra):
        total = sum0[pl.ds(first, count)].reshape(count * columns, width)
        if extra:
            total = total + incoming[pl.ds(first, count)].reshape(count * columns, width).astype(jnp.float32)
        out[0, pl.ds(first, count)] = silu(total + bias2[0]).astype(out.dtype).reshape(count, columns, width)

    @pl.when(has_prev)
    def _():
        for slot, pair in enumerate(((half - 1, half), (0, rows - 1))):
            with jax.named_scope("close%d" % slot):
                wait_bytes(pieces.at[0], q_r.at[slot])
                for row in pair:
                    close(row, 1, True)

    @pl.when(no_prev)
    def _():
        close(0, rows, False)

    with jax.named_scope("ends"):
        for copy in to_peer:
            copy.wait_send()
        for t in range(1, frames // 2):
            copy = remote(going.at[t - 1], out.at[t, theirs], o_s, o_r.at[t], peer)
            when(takes if t == 1 else None, copy.wait_recv)
        wait_bytes(v.at[pl.ds(0, frames // 2 + 1), low], o_s)

        @pl.when(has_next)
        def _():
            wait_bytes(incoming, q_s)

        @pl.when(both(one, has_next, tile == 0))
        def _():
            wait_bytes(v.at[pl.ds(0, BACK), pl.ds(0, rows)], x_s)

        @pl.when(both(one, has_next, above))
        def _():
            wait_bytes(v.at[pl.ds(0, BACK), pl.ds(0, rows + 1)], x_s)

        for condition, count in (
            (both(no_prev, has_next), 4), (both(no_prev, no_next), 3),
            (both(has_prev, has_next), 6), (both(has_prev, no_next), 5),
        ):

            @pl.when(both(one, condition))
            def _():
                wait_bytes(v.at[pl.ds(0, count), low], p_s)

        for side, condition in ((0, above), (1, below)):
            forwards = both(one, condition)
            for after, count in ((has_next, frames), (no_next, frames - 1)):
                if side == 0:

                    @pl.when(both(zero, condition, after))
                    def _():
                        wait_bytes(v.at[pl.ds(0, count), low], z_s[0])

                else:

                    @pl.when(both(forwards, after, no_prev))
                    def _():
                        wait_bytes(v.at[pl.ds(0, count), low], z_s[1])

                    @pl.when(both(forwards, after, has_prev))
                    def _():
                        wait_bytes(v.at[pl.ds(0, count + BACK), low], z_s[1])

            if side == 0:

                @pl.when(both(forwards, has_prev))
                def _():
                    wait_bytes(v.at[pl.ds(0, 1), low], z_s[0])


def shards(tiles, slabs, video, first_weight, first_bias, second_weight, second_bias):
    frames, rows, columns, channels = video.shape
    half = rows // 2
    assert half == 2 and first_weight.shape[3] == channels == second_bias.shape[0] and frames >= 4 and frames % 2 == 0
    part = first_bias.shape[0]
    width = second_bias.shape[0]
    anywhere = pl.BlockSpec(memory_space=pltpu.HBM)
    inside = pl.BlockSpec(memory_space=pltpu.VMEM)
    dma = pltpu.SemaphoreType.DMA
    vmem = pltpu.VMEM
    latents = frames // 2
    return pl.pallas_call(
        functools.partial(kernel, tiles, slabs),
        out_shape=jax.ShapeDtypeStruct((latents, rows, columns, width), jnp.bfloat16),
        in_specs=[anywhere] * 5,
        out_specs=inside,
        scratch_shapes=[
            vmem((BACK + frames, rows + 2, columns, channels), jnp.bfloat16),
            vmem((frames + 2, half + 4, columns, channels), jnp.bfloat16),
            vmem((9, 3, 2, part, channels), jnp.bfloat16),
            vmem((2, 9, 3, channels, width), jnp.bfloat16),
            vmem((2, 1, part), jnp.float32),
            vmem((2, 1, width), jnp.float32),
            vmem((2, 2, columns, width), jnp.bfloat16),
            vmem((rows, columns, width), jnp.bfloat16),
            vmem((latents - 1, half, columns, width), jnp.bfloat16),
            vmem((half, columns, width), jnp.float32),
            vmem((rows, columns, width), jnp.float32),
            vmem((2, half * columns, width), jnp.float32),
            vmem((half * columns, channels), jnp.float32),
            dma((5,)), dma, dma((2,)), dma, dma, dma((2,)), dma((2 * BACK + 1,)), dma((2,)), dma((BACK,)), dma((2,)),
            dma((latents,)),
        ],
        compiler_params=pltpu.CompilerParams(
            collective_id=0, has_side_effects=True, vmem_limit_bytes=32 << 20
        ),
    )(
        *(
            pltpu.with_memory_space_constraint(operand, pltpu.HBM)
            for operand in (
                video,
                jnp.swapaxes(first_weight, 3, 4).reshape(9, 3, part, channels),
                first_bias.reshape(1, part),
                second_weight.reshape(9, 3, channels, 2 * width),
                second_bias.reshape(1, width),
            )
        )
    )


def solution(mesh):
    placed = (
        P(("clip", "slab"), "tile", None, None),
        P(None, None, None, None, "chan"),
        P("chan"),
        P(),
        P("chan"),
    )
    return jax.shard_map(
        functools.partial(shards, mesh.shape["tile"], mesh.shape["slab"]),
        mesh=mesh,
        in_specs=placed,
        out_specs=P(("clip", "slab"), "tile", None, "chan"),
        check_vma=False,
    )
```

```python
import functools

import jax
import jax.numpy as jnp
from jax import lax
from jax.experimental import pallas as pl
from jax.experimental.pallas import tpu as pltpu
from jax.sharding import PartitionSpec as P

MESH = pl.DeviceIdType.MESH
BACK = 2


def kernel(
    tiles, slabs, video, w1, b1, w2, b2, out,
    v, h, k1, k2, bias1, bias2, pieces, incoming, going, going0, sum0, acc, acc2,
    load, w_s, b_s, z0_s, w1_r, b_r, a_r, z_r, f_r, q_r, o_r,
):
    x_s, p_s, o_s, q_s, z1_s = (load.at[n] for n in range(5))
    z_s = (z0_s, z1_s)
    frames, rows, columns, channels = video.shape
    half = rows // 2
    width = b2.shape[1]
    core = lax.axis_index("chan")
    tile = lax.axis_index("tile")
    slab = lax.axis_index("slab")
    other = 1 - core
    z_tile = tile + 2 * core - 1
    has_z = jnp.logical_and(z_tile >= 0, z_tile < tiles)
    no_z = jnp.logical_or(z_tile < 0, z_tile >= tiles)
    has_next = slab < slabs - 1
    no_next = slab == slabs - 1
    has_prev = slab > 0
    no_prev = slab == 0
    one = core == 1
    zero = core == 0
    above = tile > 0
    below = tile < tiles - 1
    peer = {"chan": other}
    z_minus = {"tile": tile - 1, "chan": 1}
    z_plus = {"tile": tile + 1, "chan": 0}
    next_same = {"slab": slab + 1}
    next_cross = {"slab": slab + 1, "chan": other}
    prev_same = {"slab": slab - 1}

    def both(*conditions):
        return functools.reduce(jnp.logical_and, conditions)

    def when(condition, body):
        if condition is None:
            body()
        else:
            pl.when(condition)(body)

    barrier = pltpu.get_barrier_semaphore()
    greetings = (
        (None, peer),
        (has_z, {"chan": other, "tile": z_tile}),
        (has_prev, {"slab": slab - 1, "chan": 1}),
        (both(one, has_prev, below), {"slab": slab - 1, "tile": tile + 1, "chan": 1}),
    )
    for condition, device in greetings:
        when(condition, lambda device=device: pl.semaphore_signal(
            barrier, inc=1, device_id=device, device_id_type=MESH))
    met = 1
    for condition, count in ((has_z, 1), (both(one, has_next), 2), (both(one, has_next, above), 1)):
        met = met + jnp.where(condition, count, 0)

    into_v = pltpu.make_async_copy(video, v.at[pl.ds(BACK, frames), pl.ds(half * other, rows)], load.at[0])
    own_w1 = pltpu.make_async_copy(w1, k1.at[:, :, core], load.at[1])
    own_b1 = pltpu.make_async_copy(b1, bias1.at[core], load.at[2])
    own_b2 = pltpu.make_async_copy(b2, bias2.at[0], load.at[4])
    own_w2 = [
        pltpu.make_async_copy(
            w2.at[:, :, :, pl.ds(pl.multiple_of(owner * width, width), width)], k2.at[n], load.at[3])
        for n, owner in enumerate((core, other))
    ]
    for copy in (into_v, own_w1, own_b1, own_b2):
        copy.start()

    def remote(src, dst, send, recv, device):
        return pltpu.make_async_remote_copy(
            src_ref=src, dst_ref=dst, send_sem=send, recv_sem=recv,
            device_id=device, device_id_type=MESH,
        )

    def wait_bytes(ref, semaphore):
        pltpu.make_async_copy(ref, ref, semaphore).wait()

    mine = pl.ds(half * core, half)
    theirs = pl.ds(half * other, half)
    halo_here = pl.ds(rows * core, half)
    frame0, frame1 = frames, frames + 1

    low, high = pl.ds(0, half), pl.ds(half, half)
    halo_low, halo_high = pl.ds(0, half), pl.ds(rows, half)

    def x_copies(device):
        return [
            [
                remote(v.at[frames + f, some], v.at[f, some], x_s, a_r.at[2 * f + n], device)
                for n, some in enumerate((low, high))
            ]
            for f in range(BACK)
        ]

    x_out = x_copies(next_same)
    x_in = x_copies(prev_same)
    slanted = remote(v.at[frames, low], v.at[0, halo_high], x_s, f_r.at[0], {"slab": slab + 1, **z_minus})
    forward_z = [
        [
            (above, remote(v.at[f, low], v.at[f, halo_high], z_s[0], f_r.at[f], z_minus)),
            (below, remote(v.at[f, high], v.at[f, halo_low], z_s[1], f_r.at[f], z_plus)),
        ]
        for f in range(BACK)
    ]
    f_in = [remote(v.at[f, low], v.at[f, halo_low], z_s[0], f_r.at[f], peer) for f in range(BACK)]
    forward_p = [remote(v.at[f, low], v.at[f, pl.ds(half, half)], p_s, a_r.at[f], peer) for f in range(BACK)]

    def share_h(index, count, place):
        return remote(
            h.at[pl.ds(index, count), low], h.at[pl.ds(index, count), pl.ds(half, half)], p_s, a_r.at[2 + place], peer
        )

    forward_h = [share_h(BACK, 1, 0), share_h(BACK + 1, 1, 1), share_h(frames, 2, 2), share_h(frames, 1, 2)]

    rest_h = [
        remote(
            h.at[pl.ds(BACK + n, n + 1), high], h.at[pl.ds(BACK + n, n + 1), pl.ds(rows, half)], o_s, a_r.at[n], peer
        )
        for n in range(2)
    ]

    def z_copies(count):
        some = pl.ds(BACK, count)
        return [
            [
                remote(video.at[pl.ds(0, count), pl.ds(n, 1)], v.at[some, pl.ds(rows + n, 1)], z_s[0], z_r.at[n], z_minus)
                for n in range(half)
            ],
            [
                remote(
                    v.at[some, pl.ds(rows - 1 - n, 1)], v.at[some, pl.ds(half - 1 - n, 1)], z_s[1], z_r.at[n], z_plus
                )
                for n in range(half)
            ],
        ]

    z_full = z_copies(frames)
    z_short = z_copies(frames - 1)

    def start_z(side):
        for condition, copies in ((has_next, z_full), (no_next, z_short)):

            @pl.when(condition)
            def _():
                for copy in copies[side]:
                    copy.start()

    to_peer = [
        remote(w1, k1.at[:, :, core], w_s, w1_r, peer),
        remote(b1, bias1.at[core], b_s.at[0], b_r.at[0], peer),
        remote(b2, bias2.at[1], b_s.at[1], b_r.at[1], peer),
    ]

    with jax.named_scope("entrybar"):
        pl.semaphore_wait(barrier, met)

    @pl.when(both(zero, above))
    def _():
        start_z(0)

    for copy in to_peer:
        copy.start()
    with jax.named_scope("loadwait"):
        into_v.wait()
        own_w1.wait()
        own_b1.wait()
        own_b2.wait()

    @pl.when(one)
    def _():
        @pl.when(has_next)
        def _():
            for f, n in ((1, 0), (1, 1), (0, 1), (0, 0)):
                x_out[f][n].start()

        @pl.when(below)
        def _():
            start_z(1)

    for copy in own_w2:
        copy.start()

    @pl.when(no_z)
    def _():
        v[:, halo_here] = jnp.zeros((v.shape[0], half, columns, channels), v.dtype)

    def taps(source, index, first, count, steps):
        return jnp.concatenate(
            [
                source[index + a, pl.ds(first + b, count)].reshape(count * columns, channels)
                for a in steps
                for b in range(3)
            ],
            axis=1,
        )

    def shifted(parts, size):
        column = lax.broadcasted_iota(jnp.int32, (parts.shape[0], size), 0) % columns
        before = pltpu.roll(parts[:, 0:size], 1, 0)
        after = pltpu.roll(parts[:, 2 * size : 3 * size], parts.shape[0] - 1, 0)
        total = parts[:, size : 2 * size] + jnp.where(column == 0, 0.0, before)
        return total + jnp.where(column == columns - 1, 0.0, after)

    def silu(total):
        return total / (1.0 + jnp.exp(-total))

    def hidden_sum(indices, first, count, steps):
        parts = lax.dot_general(
            jnp.concatenate([taps(v, index - 2, first, count, steps) for index in indices], axis=0),
            jnp.concatenate(
                [k1[3 * a + b].reshape(3 * channels, channels) for a in steps for b in range(3)], axis=1
            ),
            (((1,), (1,)), ((), ())),
            preferred_element_type=jnp.float32,
        )
        return shifted(parts, channels)

    no_rows = {"inner": (), "near": (), "far": (no_z,), "outer": (both(no_z, zero), both(no_z, one))}

    def hidden(kind, indices, first, count, oldest=0, newest=2, before=None):
        total = hidden_sum(indices, first, count, range(oldest, newest + 1))
        if before is not None:
            total = total + before
        bias = jnp.concatenate([bias1[0], bias1[1]], axis=1)
        value = silu(total + bias)
        value = value.reshape(len(indices), count, columns, channels)
        for n, index in enumerate(indices):
            new = value[n]
            if no_rows[kind]:
                new = jnp.stack([jnp.where(no_rows[kind][row], 0.0, new[row]) for row in range(count)])
            h[index, pl.ds(first, count)] = new.astype(h.dtype)

    def inner(*indices, oldest=0):
        with jax.named_scope("inner" + "_".join(map(str, indices))):
            hidden("inner", indices, half * other, half, oldest)

    def outer(*indices, oldest=0):
        with jax.named_scope("outer" + "_".join(map(str, indices))):
            hidden("outer", indices, half * core, half, oldest)

    def near(*indices, oldest=0):
        with jax.named_scope("near" + "_".join(map(str, indices))):
            hidden("near", indices, 1 + core, 1, oldest)

    def far(*indices, oldest=0):
        with jax.named_scope("far" + "_".join(map(str, indices))):
            hidden("far", indices, (rows - 1) * core, 1, oldest)

    def outer_begin(index):
        with jax.named_scope("outer%da" % index):
            acc2[...] = hidden_sum((index,), half * core, half, range(1, 3))

    def outer_end(index):
        with jax.named_scope("outer%db" % index):
            hidden("outer", (index,), half * core, half, 0, 0, acc2[...])

    def second(index, first, count, steps, blocks):
        matrix = jnp.concatenate(
            [
                jnp.concatenate([k2[n, 3 * (a + shift) + b, e] for n, shift in blocks for e in range(3)], axis=1)
                for a in steps
                for b in range(3)
            ],
            axis=0,
        )
        parts = jnp.dot(taps(h, index, first, count, steps), matrix, preferred_element_type=jnp.float32)
        return [shifted(parts[:, 3 * k * width : 3 * (k + 1) * width], width) for k in range(len(blocks))]

    whole = ((0, 0), (1, 0))

    def share(slot, local):
        place = half * core + local
        return [
            remote(pieces.at[slot, 0], incoming.at[place], q_s, q_r.at[slot], next_same),
            remote(pieces.at[slot, 1], incoming.at[place], q_s, q_r.at[slot], next_cross),
        ]

    shares = [share(0, other), share(1, core)]

    def send_share(slot, local):
        with jax.named_scope("share%d" % slot):
            halves = second(frames, local, 1, range(0, 2), whole)
            for n in (1, 0):
                pieces[slot, n] = halves[n].astype(pieces.dtype)
                shares[slot][n].start()

    result = [
        remote(going.at[t - 1], out.at[t, mine], o_s, o_r.at[t], peer) for t in range(1, frames // 2)
    ]
    part0 = remote(going0, sum0.at[mine], o_s, o_r.at[0], peer)

    def latent(t):
        with jax.named_scope("latent%d" % t):
            own, away = second(2 * t, 0, half, range(3), whole)
            going[t - 1] = silu(away + bias2[1]).astype(out.dtype).reshape(half, columns, width)
            result[t - 1].start()
            out[t, mine] = silu(own + bias2[0]).astype(out.dtype).reshape(half, columns, width)

    def later_steps(steps=range(1, 3), start=True):
        with jax.named_scope("latent1a%d" % len(steps)):
            halves = second(2, 0, half, steps, whole)
            for n in range(2):
                acc[n] = halves[n] if start else acc[n] + halves[n]

    def own_steps(first):
        place = pl.ds(half * core if first == 0 else half, half)
        with jax.named_scope("own1a"):
            acc[0] = second(2, first, half, range(1, 3), ((0, 0),))[0]
        with jax.named_scope("own"):
            one_sum, then = second(2, first, half, range(0, 1), ((0, 2), (0, 0)))
            sum0[place] = one_sum.reshape(half, columns, width)
            out[1, place] = silu(then + acc[0] + bias2[0]).astype(out.dtype).reshape(half, columns, width)

    def last_steps():
        with jax.named_scope("tailA"):
            first, then = second(2, 0, half, range(0, 1), ((1, 2), (1, 0)))
            going0[...] = first.reshape(half, columns, width)
            part0.start()
            going[0] = silu(then + acc[1] + bias2[1]).astype(out.dtype).reshape(half, columns, width)
            result[0].start()
        with jax.named_scope("tailB"):
            first, then = second(2, 0, half, range(0, 1), ((0, 2), (0, 0)))
            sum0[mine] = first.reshape(half, columns, width)
            out[1, mine] = silu(then + acc[0] + bias2[0]).astype(out.dtype).reshape(half, columns, width)

    def wait_z(which, copies):
        with jax.named_scope("zwait%d" % which):

            @pl.when(has_z)
            def _():
                copies[0][which].wait_recv()

    def pass_on(f, n):
        with jax.named_scope("pass%d%d" % (f, n)):
            x_in[f][n].wait_recv()
            condition, copy = forward_z[f][n]
            if (f, n) != (0, 0):
                pl.when(condition)(copy.start)
            if n == 0:
                forward_p[f].start()

    def from_peer(name, copy):
        @pl.when(zero)
        def _():
            with jax.named_scope(name):
                copy.wait_recv()

    def halo_ready(name, copy):
        with jax.named_scope(name):

            @pl.when(has_z)
            def _():
                copy.wait_recv()

    def w2_ready():
        with jax.named_scope("w2wait"):
            wait_bytes(k2, load.at[3])

    with jax.named_scope("w1wait"):
        remote(w1, k1.at[:, :, other], w_s, w1_r, peer).wait_recv()
        remote(b1, bias1.at[other], b_s.at[0], b_r.at[0], peer).wait_recv()
        to_peer[2].wait_recv()

    last = frames + 1

    @pl.when(both(one, has_next))
    def _():
        inner(frames, last)
        forward_h[2].start()

    @pl.when(both(one, no_next))
    def _():
        inner(frames)
        forward_h[3].start()

    @pl.when(both(one, no_prev))
    def _():
        inner(3, oldest=1)
        forward_h[1].start()
        inner(2, oldest=2)
        forward_h[0].start()

    @pl.when(both(one, has_next, above))
    def _():
        slanted.start()

    @pl.when(has_next)
    def _():
        wait_z(0, z_full)
        near(frames, last)
        w2_ready()
        from_peer("hwait2", forward_h[2])
        send_share(0, other)

        wait_z(1, z_full)

        @pl.when(jnp.logical_or(above, has_prev))
        def _():
            far(frames, last)
            send_share(1, core)

    def middle():
        for index in range(frames - 1, 3, -1):
            inner(index)
            outer(index)
        for t in range(2, frames // 2):
            latent(t)

    def own_last():
        @pl.when(no_next)
        def _():
            wait_z(0, z_short)
            wait_z(1, z_short)
            outer(frames)

    def own_ready():
        @pl.when(no_next)
        def _():
            w2_ready()
            from_peer("hwait2", forward_h[3])

    @pl.when(no_prev)
    def _():
        own_last()
        own_ready()
        middle()

        @pl.when(both(has_next, tile == 0))
        def _():
            far(frames, last)
            outer(3, oldest=1)
            outer(2, oldest=2)

        @pl.when(jnp.logical_or(above, no_next))
        def _():
            outer(3, oldest=1)
            outer(2, oldest=2)

        @pl.when(one)
        def _():
            rest_h[1].start()
            rest_h[0].start()

        @pl.when(both(has_next, tile == 0))
        def _():
            send_share(1, core)

        @pl.when(one)
        def _():
            own_steps(0)

        @pl.when(zero)
        def _():
            forward_h[1].wait_recv()
            forward_h[0].wait_recv()
            later_steps()
            last_steps()
            for copy in rest_h:
                copy.wait_recv()
            own_steps(half)

    @pl.when(has_prev)
    def _():
        @pl.when(one)
        def _():
            pass_on(1, 0)
            pass_on(1, 1)
            inner(3)
            forward_h[1].start()
            pass_on(0, 1)
            own_last()
            pass_on(0, 0)
            inner(2)
            forward_h[0].start()

        @pl.when(zero)
        def _():
            own_last()

        own_ready()
        middle()
        later_steps(range(2, 3))
        from_peer("pwait1", forward_p[1])
        halo_ready("fwait1", f_in[1])
        from_peer("hwait1", forward_h[1])
        outer(3)
        later_steps(range(1, 2), False)
        outer_begin(2)
        from_peer("pwait0", forward_p[0])
        from_peer("hwait0", forward_h[0])
        halo_ready("fwait0", f_in[0])
        outer_end(2)
        last_steps()


    takes = jnp.logical_or(has_prev, one)

    @pl.when(takes)
    def _():
        remote(going0, sum0.at[theirs], o_s, o_r.at[0], peer).wait_recv()

    def close(first, count, extra):
        total = sum0[pl.ds(first, count)].reshape(count * columns, width)
        if extra:
            total = total + incoming[pl.ds(first, count)].reshape(count * columns, width).astype(jnp.float32)
        out[0, pl.ds(first, count)] = silu(total + bias2[0]).astype(out.dtype).reshape(count, columns, width)

    @pl.when(has_prev)
    def _():
        for slot, pair in enumerate(((half - 1, half), (0, rows - 1))):
            with jax.named_scope("close%d" % slot):
                wait_bytes(pieces.at[0], q_r.at[slot])
                for row in pair:
                    close(row, 1, True)

    @pl.when(no_prev)
    def _():
        close(0, rows, False)

    with jax.named_scope("ends"):
        for copy in to_peer:
            copy.wait_send()
        for t in range(1, frames // 2):
            copy = remote(going.at[t - 1], out.at[t, theirs], o_s, o_r.at[t], peer)
            when(takes if t == 1 else None, copy.wait_recv)
        wait_bytes(v.at[pl.ds(0, frames // 2 + 1), low], o_s)

        @pl.when(has_next)
        def _():
            wait_bytes(incoming, q_s)

        @pl.when(both(one, has_next, tile == 0))
        def _():
            wait_bytes(v.at[pl.ds(0, BACK), pl.ds(0, rows)], x_s)

        @pl.when(both(one, has_next, above))
        def _():
            wait_bytes(v.at[pl.ds(0, BACK), pl.ds(0, rows + 1)], x_s)

        for condition, count in (
            (both(no_prev, has_next), 4), (both(no_prev, no_next), 3),
            (both(has_prev, has_next), 6), (both(has_prev, no_next), 5),
        ):

            @pl.when(both(one, condition))
            def _():
                wait_bytes(v.at[pl.ds(0, count), low], p_s)

        for side, condition in ((0, above), (1, below)):
            forwards = both(one, condition)
            for after, count in ((has_next, frames), (no_next, frames - 1)):
                if side == 0:

                    @pl.when(both(zero, condition, after))
                    def _():
                        wait_bytes(v.at[pl.ds(0, count), low], z_s[0])

                else:

                    @pl.when(both(forwards, after, no_prev))
                    def _():
                        wait_bytes(v.at[pl.ds(0, count), low], z_s[1])

                    @pl.when(both(forwards, after, has_prev))
                    def _():
                        wait_bytes(v.at[pl.ds(0, count + BACK), low], z_s[1])

            if side == 0:

                @pl.when(both(forwards, has_prev))
                def _():
                    wait_bytes(v.at[pl.ds(0, 1), low], z_s[0])


def shards(tiles, slabs, video, first_weight, first_bias, second_weight, second_bias):
    frames, rows, columns, channels = video.shape
    half = rows // 2
    assert half == 2 and first_weight.shape[3] == channels == second_bias.shape[0] and frames >= 4 and frames % 2 == 0
    part = first_bias.shape[0]
    width = second_bias.shape[0]
    anywhere = pl.BlockSpec(memory_space=pltpu.HBM)
    inside = pl.BlockSpec(memory_space=pltpu.VMEM)
    dma = pltpu.SemaphoreType.DMA
    vmem = pltpu.VMEM
    latents = frames // 2
    return pl.pallas_call(
        functools.partial(kernel, tiles, slabs),
        out_shape=jax.ShapeDtypeStruct((latents, rows, columns, width), jnp.bfloat16),
        in_specs=[anywhere] * 5,
        out_specs=inside,
        scratch_shapes=[
            vmem((BACK + frames, rows + 2, columns, channels), jnp.bfloat16),
            vmem((frames + 2, half + 4, columns, channels), jnp.bfloat16),
            vmem((9, 3, 2, part, channels), jnp.bfloat16),
            vmem((2, 9, 3, channels, width), jnp.bfloat16),
            vmem((2, 1, part), jnp.float32),
            vmem((2, 1, width), jnp.float32),
            vmem((2, 2, columns, width), jnp.bfloat16),
            vmem((rows, columns, width), jnp.bfloat16),
            vmem((latents - 1, half, columns, width), jnp.bfloat16),
            vmem((half, columns, width), jnp.float32),
            vmem((rows, columns, width), jnp.float32),
            vmem((2, half * columns, width), jnp.float32),
            vmem((half * columns, channels), jnp.float32),
            dma((5,)), dma, dma((2,)), dma, dma, dma((2,)), dma((2 * BACK + 1,)), dma((2,)), dma((BACK,)), dma((2,)),
            dma((latents,)),
        ],
        compiler_params=pltpu.CompilerParams(
            collective_id=0, has_side_effects=True, vmem_limit_bytes=32 << 20
        ),
    )(
        *(
            pltpu.with_memory_space_constraint(operand, pltpu.HBM)
            for operand in (
                video,
                jnp.swapaxes(first_weight, 3, 4).reshape(9, 3, part, channels),
                first_bias.reshape(1, part),
                second_weight.reshape(9, 3, channels, 2 * width),
                second_bias.reshape(1, width),
            )
        )
    )


def solution(mesh):
    placed = (
        P(("clip", "slab"), "tile", None, None),
        P(None, None, None, None, "chan"),
        P("chan"),
        P(),
        P("chan"),
    )
    return jax.shard_map(
        functools.partial(shards, mesh.shape["tile"], mesh.shape["slab"]),
        mesh=mesh,
        in_specs=placed,
        out_specs=P(("clip", "slab"), "tile", None, "chan"),
        check_vma=False,
    )
```

```python
import functools

import jax
import jax.numpy as jnp
from jax import lax
from jax.experimental import pallas as pl
from jax.experimental.pallas import tpu as pltpu
from jax.sharding import PartitionSpec as P

MESH = pl.DeviceIdType.MESH
BACK = 2


def kernel(
    tiles, slabs, video, w1, b1, w2, b2, out,
    v, h, k1, k2, bias1, bias2, pieces, incoming, going, going0, sum0, acc, acc2,
    load, w_s, b_s, z0_s, w1_r, b_r, a_r, z_r, f_r, q_r, o_r,
):
    x_s, p_s, o_s, q_s, z1_s = (load.at[n] for n in range(5))
    z_s = (z0_s, z1_s)
    frames, rows, columns, channels = video.shape
    half = rows // 2
    width = b2.shape[1]
    core = lax.axis_index("chan")
    tile = lax.axis_index("tile")
    slab = lax.axis_index("slab")
    other = 1 - core
    z_tile = tile + 2 * core - 1
    has_z = jnp.logical_and(z_tile >= 0, z_tile < tiles)
    no_z = jnp.logical_or(z_tile < 0, z_tile >= tiles)
    has_next = slab < slabs - 1
    no_next = slab == slabs - 1
    has_prev = slab > 0
    no_prev = slab == 0
    one = core == 1
    zero = core == 0
    above = tile > 0
    below = tile < tiles - 1
    peer = {"chan": other}
    z_minus = {"tile": tile - 1, "chan": 1}
    z_plus = {"tile": tile + 1, "chan": 0}
    next_same = {"slab": slab + 1}
    next_cross = {"slab": slab + 1, "chan": other}
    prev_same = {"slab": slab - 1}

    def both(*conditions):
        return functools.reduce(jnp.logical_and, conditions)

    def when(condition, body):
        if condition is None:
            body()
        else:
            pl.when(condition)(body)

    barrier = pltpu.get_barrier_semaphore()
    greetings = (
        (None, peer),
        (has_z, {"chan": other, "tile": z_tile}),
        (has_prev, {"slab": slab - 1, "chan": 1}),
        (both(one, has_prev, below), {"slab": slab - 1, "tile": tile + 1, "chan": 1}),
    )
    for condition, device in greetings:
        when(condition, lambda device=device: pl.semaphore_signal(
            barrier, inc=1, device_id=device, device_id_type=MESH))
    met = 1
    for condition, count in ((has_z, 1), (both(one, has_next), 2), (both(one, has_next, above), 1)):
        met = met + jnp.where(condition, count, 0)

    into_v = pltpu.make_async_copy(video, v.at[pl.ds(BACK, frames), pl.ds(half * other, rows)], load.at[0])
    own_w1 = pltpu.make_async_copy(w1, k1.at[:, :, core], load.at[1])
    own_b1 = pltpu.make_async_copy(b1, bias1.at[core], load.at[2])
    own_b2 = pltpu.make_async_copy(b2, bias2.at[0], load.at[4])
    own_w2 = [
        pltpu.make_async_copy(
            w2.at[:, :, :, pl.ds(pl.multiple_of(owner * width, width), width)], k2.at[n], load.at[3])
        for n, owner in enumerate((core, other))
    ]
    for copy in (into_v, own_w1, own_b1, own_b2):
        copy.start()

    def remote(src, dst, send, recv, device):
        return pltpu.make_async_remote_copy(
            src_ref=src, dst_ref=dst, send_sem=send, recv_sem=recv,
            device_id=device, device_id_type=MESH,
        )

    def wait_bytes(ref, semaphore):
        pltpu.make_async_copy(ref, ref, semaphore).wait()

    mine = pl.ds(half * core, half)
    theirs = pl.ds(half * other, half)
    halo_here = pl.ds(rows * core, half)
    frame0, frame1 = frames, frames + 1

    low, high = pl.ds(0, half), pl.ds(half, half)
    halo_low, halo_high = pl.ds(0, half), pl.ds(rows, half)

    def x_copies(device):
        return [
            [
                remote(v.at[frames + f, some], v.at[f, some], x_s, a_r.at[2 * f + n], device)
                for n, some in enumerate((low, high))
            ]
            for f in range(BACK)
        ]

    x_out = x_copies(next_same)
    x_in = x_copies(prev_same)
    slanted = remote(v.at[frames, low], v.at[0, halo_high], x_s, f_r.at[0], {"slab": slab + 1, **z_minus})
    forward_z = [
        [
            (above, remote(v.at[f, low], v.at[f, halo_high], z_s[0], f_r.at[f], z_minus)),
            (below, remote(v.at[f, high], v.at[f, halo_low], z_s[1], f_r.at[f], z_plus)),
        ]
        for f in range(BACK)
    ]
    f_in = [remote(v.at[f, low], v.at[f, halo_low], z_s[0], f_r.at[f], peer) for f in range(BACK)]
    forward_p = [remote(v.at[f, low], v.at[f, pl.ds(half, half)], p_s, a_r.at[f], peer) for f in range(BACK)]

    def share_h(index, count, place):
        return remote(
            h.at[pl.ds(index, count), low], h.at[pl.ds(index, count), pl.ds(half, half)], p_s, a_r.at[2 + place], peer
        )

    forward_h = [share_h(BACK, 1, 0), share_h(BACK + 1, 1, 1), share_h(frames, 2, 2), share_h(frames, 1, 2)]

    rest_h = [
        remote(
            h.at[pl.ds(BACK + n, n + 1), high], h.at[pl.ds(BACK + n, n + 1), pl.ds(rows, half)], o_s, a_r.at[n], peer
        )
        for n in range(2)
    ]

    def z_copies(count):
        some = pl.ds(BACK, count)
        return [
            [
                remote(video.at[pl.ds(0, count), pl.ds(n, 1)], v.at[some, pl.ds(rows + n, 1)], z_s[0], z_r.at[n], z_minus)
                for n in range(half)
            ],
            [
                remote(
                    v.at[some, pl.ds(rows - 1 - n, 1)], v.at[some, pl.ds(half - 1 - n, 1)], z_s[1], z_r.at[n], z_plus
                )
                for n in range(half)
            ],
        ]

    z_full = z_copies(frames)
    z_short = z_copies(frames - 1)

    def start_z(side):
        for condition, copies in ((has_next, z_full), (no_next, z_short)):

            @pl.when(condition)
            def _():
                for copy in copies[side]:
                    copy.start()

    to_peer = [
        remote(w1, k1.at[:, :, core], w_s, w1_r, peer),
        remote(b1, bias1.at[core], b_s.at[0], b_r.at[0], peer),
        remote(b2, bias2.at[1], b_s.at[1], b_r.at[1], peer),
    ]

    with jax.named_scope("entrybar"):
        pl.semaphore_wait(barrier, met)

    @pl.when(both(zero, above))
    def _():
        start_z(0)

    for copy in to_peer:
        copy.start()
    with jax.named_scope("loadwait"):
        into_v.wait()
        own_w1.wait()
        own_b1.wait()
        own_b2.wait()

    @pl.when(one)
    def _():
        @pl.when(has_next)
        def _():
            for f, n in ((1, 0), (1, 1), (0, 1), (0, 0)):
                x_out[f][n].start()

        @pl.when(below)
        def _():
            start_z(1)

    for copy in own_w2:
        copy.start()

    @pl.when(no_z)
    def _():
        v[:, halo_here] = jnp.zeros((v.shape[0], half, columns, channels), v.dtype)

    def taps(source, index, first, count, steps):
        return jnp.concatenate(
            [
                source[index + a, pl.ds(first + b, count)].reshape(count * columns, channels)
                for a in steps
                for b in range(3)
            ],
            axis=1,
        )

    def shifted(parts, size):
        column = lax.broadcasted_iota(jnp.int32, (parts.shape[0], size), 0) % columns
        before = pltpu.roll(parts[:, 0:size], 1, 0)
        after = pltpu.roll(parts[:, 2 * size : 3 * size], parts.shape[0] - 1, 0)
        total = parts[:, size : 2 * size] + jnp.where(column == 0, 0.0, before)
        return total + jnp.where(column == columns - 1, 0.0, after)

    def silu(total):
        return total / (1.0 + jnp.exp(-total))

    def hidden_sum(indices, first, count, steps):
        parts = lax.dot_general(
            jnp.concatenate([taps(v, index - 2, first, count, steps) for index in indices], axis=0),
            jnp.concatenate(
                [k1[3 * a + b].reshape(3 * channels, channels) for a in steps for b in range(3)], axis=1
            ),
            (((1,), (1,)), ((), ())),
            preferred_element_type=jnp.float32,
        )
        return shifted(parts, channels)

    no_rows = {"inner": (), "near": (), "far": (no_z,), "outer": (both(no_z, zero), both(no_z, one))}

    def hidden(kind, indices, first, count, oldest=0, newest=2, before=None):
        total = hidden_sum(indices, first, count, range(oldest, newest + 1))
        if before is not None:
            total = total + before
        bias = jnp.concatenate([bias1[0], bias1[1]], axis=1)
        value = silu(total + bias)
        value = value.reshape(len(indices), count, columns, channels)
        for n, index in enumerate(indices):
            new = value[n]
            if no_rows[kind]:
                new = jnp.stack([jnp.where(no_rows[kind][row], 0.0, new[row]) for row in range(count)])
            h[index, pl.ds(first, count)] = new.astype(h.dtype)

    def inner(*indices, oldest=0):
        with jax.named_scope("inner" + "_".join(map(str, indices))):
            hidden("inner", indices, half * other, half, oldest)

    def outer(*indices, oldest=0):
        with jax.named_scope("outer" + "_".join(map(str, indices))):
            hidden("outer", indices, half * core, half, oldest)

    def near(*indices, oldest=0):
        with jax.named_scope("near" + "_".join(map(str, indices))):
            hidden("near", indices, 1 + core, 1, oldest)

    def far(*indices, oldest=0):
        with jax.named_scope("far" + "_".join(map(str, indices))):
            hidden("far", indices, (rows - 1) * core, 1, oldest)

    def outer_begin(index):
        with jax.named_scope("outer%da" % index):
            acc2[...] = hidden_sum((index,), half * core, half, range(1, 3))

    def outer_end(index):
        with jax.named_scope("outer%db" % index):
            hidden("outer", (index,), half * core, half, 0, 0, acc2[...])

    def second(index, first, count, steps, blocks):
        matrix = jnp.concatenate(
            [
                jnp.concatenate([k2[n, 3 * (a + shift) + b, e] for n, shift in blocks for e in range(3)], axis=1)
                for a in steps
                for b in range(3)
            ],
            axis=0,
        )
        parts = jnp.dot(taps(h, index, first, count, steps), matrix, preferred_element_type=jnp.float32)
        return [shifted(parts[:, 3 * k * width : 3 * (k + 1) * width], width) for k in range(len(blocks))]

    whole = ((0, 0), (1, 0))

    def share(slot, local):
        place = half * core + local
        return [
            remote(pieces.at[slot, 0], incoming.at[place], q_s, q_r.at[slot], next_same),
            remote(pieces.at[slot, 1], incoming.at[place], q_s, q_r.at[slot], next_cross),
        ]

    shares = [share(0, other), share(1, core)]

    def send_share(slot, local):
        with jax.named_scope("share%d" % slot):
            halves = second(frames, local, 1, range(0, 2), whole)
            for n in (1, 0):
                pieces[slot, n] = halves[n].astype(pieces.dtype)
                shares[slot][n].start()

    result = [
        remote(going.at[t - 1], out.at[t, mine], o_s, o_r.at[t], peer) for t in range(1, frames // 2)
    ]
    part0 = remote(going0, sum0.at[mine], o_s, o_r.at[0], peer)

    def latent(t):
        with jax.named_scope("latent%d" % t):
            own, away = second(2 * t, 0, half, range(3), whole)
            going[t - 1] = silu(away + bias2[1]).astype(out.dtype).reshape(half, columns, width)
            result[t - 1].start()
            out[t, mine] = silu(own + bias2[0]).astype(out.dtype).reshape(half, columns, width)

    def later_steps(steps=range(1, 3), start=True):
        with jax.named_scope("latent1a%d" % len(steps)):
            halves = second(2, 0, half, steps, whole)
            for n in range(2):
                acc[n] = halves[n] if start else acc[n] + halves[n]

    def own_steps(first):
        place = pl.ds(half * core if first == 0 else half, half)
        with jax.named_scope("own1a"):
            acc[0] = second(2, first, half, range(1, 3), ((0, 0),))[0]
        with jax.named_scope("own"):
            one_sum, then = second(2, first, half, range(0, 1), ((0, 2), (0, 0)))
            sum0[place] = one_sum.reshape(half, columns, width)
            out[1, place] = silu(then + acc[0] + bias2[0]).astype(out.dtype).reshape(half, columns, width)

    def last_steps():
        with jax.named_scope("tailA"):
            first, then = second(2, 0, half, range(0, 1), ((1, 2), (1, 0)))
            going0[...] = first.reshape(half, columns, width)
            part0.start()
            going[0] = silu(then + acc[1] + bias2[1]).astype(out.dtype).reshape(half, columns, width)
            result[0].start()
        with jax.named_scope("tailB"):
            first, then = second(2, 0, half, range(0, 1), ((0, 2), (0, 0)))
            sum0[mine] = first.reshape(half, columns, width)
            out[1, mine] = silu(then + acc[0] + bias2[0]).astype(out.dtype).reshape(half, columns, width)

    def wait_z(which, copies):
        with jax.named_scope("zwait%d" % which):

            @pl.when(has_z)
            def _():
                copies[0][which].wait_recv()

    def pass_on(f, n):
        with jax.named_scope("pass%d%d" % (f, n)):
            x_in[f][n].wait_recv()
            condition, copy = forward_z[f][n]
            if (f, n) != (0, 0):
                pl.when(condition)(copy.start)
            if n == 0:
                forward_p[f].start()

    def from_peer(name, copy):
        @pl.when(zero)
        def _():
            with jax.named_scope(name):
                copy.wait_recv()

    def halo_ready(name, copy):
        with jax.named_scope(name):

            @pl.when(has_z)
            def _():
                copy.wait_recv()

    def w2_ready():
        with jax.named_scope("w2wait"):
            wait_bytes(k2, load.at[3])

    with jax.named_scope("w1wait"):
        remote(w1, k1.at[:, :, other], w_s, w1_r, peer).wait_recv()
        remote(b1, bias1.at[other], b_s.at[0], b_r.at[0], peer).wait_recv()
        to_peer[2].wait_recv()

    last = frames + 1

    @pl.when(both(one, has_next))
    def _():
        inner(frames, last)
        forward_h[2].start()

    @pl.when(both(one, no_next))
    def _():
        inner(frames)
        forward_h[3].start()

    @pl.when(both(one, no_prev))
    def _():
        inner(3, oldest=1)
        forward_h[1].start()
        inner(2, oldest=2)
        forward_h[0].start()

    @pl.when(both(one, has_next, above))
    def _():
        slanted.start()

    @pl.when(has_next)
    def _():
        wait_z(0, z_full)
        near(frames, last)
        w2_ready()
        from_peer("hwait2", forward_h[2])
        send_share(0, other)

        wait_z(1, z_full)

        @pl.when(jnp.logical_or(above, has_prev))
        def _():
            far(frames, last)
            send_share(1, core)

    def middle():
        for index in range(frames - 1, 3, -1):
            inner(index)
            outer(index)
        for t in range(2, frames // 2):
            latent(t)

    def own_last():
        @pl.when(no_next)
        def _():
            wait_z(0, z_short)
            wait_z(1, z_short)
            outer(frames)

    def own_ready():
        @pl.when(no_next)
        def _():
            w2_ready()
            from_peer("hwait2", forward_h[3])

    @pl.when(no_prev)
    def _():
        own_last()
        own_ready()
        middle()

        @pl.when(both(has_next, tile == 0))
        def _():
            far(frames, last)
            outer(3, oldest=1)
            outer(2, oldest=2)

        @pl.when(jnp.logical_or(above, no_next))
        def _():
            outer(3, oldest=1)
            outer(2, oldest=2)

        @pl.when(one)
        def _():
            rest_h[1].start()
            rest_h[0].start()

        @pl.when(both(has_next, tile == 0))
        def _():
            send_share(1, core)

        @pl.when(one)
        def _():
            own_steps(0)

        @pl.when(zero)
        def _():
            forward_h[1].wait_recv()
            forward_h[0].wait_recv()
            later_steps()
            last_steps()
            for copy in rest_h:
                copy.wait_recv()
            own_steps(half)

    @pl.when(has_prev)
    def _():
        @pl.when(one)
        def _():
            pass_on(1, 0)
            pass_on(1, 1)
            inner(3)
            forward_h[1].start()
            pass_on(0, 1)
            own_last()
            pass_on(0, 0)
            inner(2)
            forward_h[0].start()

        @pl.when(zero)
        def _():
            own_last()

        own_ready()
        middle()
        later_steps(range(2, 3))
        @pl.when(one)
        def _():
            halo_ready("fwait1", f_in[1])
            halo_ready("fwait0", f_in[0])
            outer(3)
            outer(2)
            later_steps(range(1, 2), False)
            last_steps()

        @pl.when(zero)
        def _():
            forward_p[1].wait_recv()
            halo_ready("fwait1", f_in[1])
            forward_h[1].wait_recv()
            outer(3)
            later_steps(range(1, 2), False)
            outer_begin(2)
            forward_p[0].wait_recv()
            forward_h[0].wait_recv()
            halo_ready("fwait0", f_in[0])
            outer_end(2)
            last_steps()


    takes = jnp.logical_or(has_prev, one)

    @pl.when(takes)
    def _():
        remote(going0, sum0.at[theirs], o_s, o_r.at[0], peer).wait_recv()

    def close(first, count, extra):
        total = sum0[pl.ds(first, count)].reshape(count * columns, width)
        if extra:
            total = total + incoming[pl.ds(first, count)].reshape(count * columns, width).astype(jnp.float32)
        out[0, pl.ds(first, count)] = silu(total + bias2[0]).astype(out.dtype).reshape(count, columns, width)

    @pl.when(has_prev)
    def _():
        for slot, pair in enumerate(((half - 1, half), (0, rows - 1))):
            with jax.named_scope("close%d" % slot):
                wait_bytes(pieces.at[0], q_r.at[slot])
                for row in pair:
                    close(row, 1, True)

    @pl.when(no_prev)
    def _():
        close(0, rows, False)

    with jax.named_scope("ends"):
        for copy in to_peer:
            copy.wait_send()
        for t in range(1, frames // 2):
            copy = remote(going.at[t - 1], out.at[t, theirs], o_s, o_r.at[t], peer)
            when(takes if t == 1 else None, copy.wait_recv)
        wait_bytes(v.at[pl.ds(0, frames // 2 + 1), low], o_s)

        @pl.when(has_next)
        def _():
            wait_bytes(incoming, q_s)

        @pl.when(both(one, has_next, tile == 0))
        def _():
            wait_bytes(v.at[pl.ds(0, BACK), pl.ds(0, rows)], x_s)

        @pl.when(both(one, has_next, above))
        def _():
            wait_bytes(v.at[pl.ds(0, BACK), pl.ds(0, rows + 1)], x_s)

        for condition, count in (
            (both(no_prev, has_next), 4), (both(no_prev, no_next), 3),
            (both(has_prev, has_next), 6), (both(has_prev, no_next), 5),
        ):

            @pl.when(both(one, condition))
            def _():
                wait_bytes(v.at[pl.ds(0, count), low], p_s)

        for side, condition in ((0, above), (1, below)):
            forwards = both(one, condition)
            for after, count in ((has_next, frames), (no_next, frames - 1)):
                if side == 0:

                    @pl.when(both(zero, condition, after))
                    def _():
                        wait_bytes(v.at[pl.ds(0, count), low], z_s[0])

                else:

                    @pl.when(both(forwards, after, no_prev))
                    def _():
                        wait_bytes(v.at[pl.ds(0, count), low], z_s[1])

                    @pl.when(both(forwards, after, has_prev))
                    def _():
                        wait_bytes(v.at[pl.ds(0, count + BACK), low], z_s[1])

            if side == 0:

                @pl.when(both(forwards, has_prev))
                def _():
                    wait_bytes(v.at[pl.ds(0, 1), low], z_s[0])


def shards(tiles, slabs, video, first_weight, first_bias, second_weight, second_bias):
    frames, rows, columns, channels = video.shape
    half = rows // 2
    assert half == 2 and first_weight.shape[3] == channels == second_bias.shape[0] and frames >= 4 and frames % 2 == 0
    part = first_bias.shape[0]
    width = second_bias.shape[0]
    anywhere = pl.BlockSpec(memory_space=pltpu.HBM)
    inside = pl.BlockSpec(memory_space=pltpu.VMEM)
    dma = pltpu.SemaphoreType.DMA
    vmem = pltpu.VMEM
    latents = frames // 2
    return pl.pallas_call(
        functools.partial(kernel, tiles, slabs),
        out_shape=jax.ShapeDtypeStruct((latents, rows, columns, width), jnp.bfloat16),
        in_specs=[anywhere] * 5,
        out_specs=inside,
        scratch_shapes=[
            vmem((BACK + frames, rows + 2, columns, channels), jnp.bfloat16),
            vmem((frames + 2, half + 4, columns, channels), jnp.bfloat16),
            vmem((9, 3, 2, part, channels), jnp.bfloat16),
            vmem((2, 9, 3, channels, width), jnp.bfloat16),
            vmem((2, 1, part), jnp.float32),
            vmem((2, 1, width), jnp.float32),
            vmem((2, 2, columns, width), jnp.bfloat16),
            vmem((rows, columns, width), jnp.bfloat16),
            vmem((latents - 1, half, columns, width), jnp.bfloat16),
            vmem((half, columns, width), jnp.float32),
            vmem((rows, columns, width), jnp.float32),
            vmem((2, half * columns, width), jnp.float32),
            vmem((half * columns, channels), jnp.float32),
            dma((5,)), dma, dma((2,)), dma, dma, dma((2,)), dma((2 * BACK + 1,)), dma((2,)), dma((BACK,)), dma((2,)),
            dma((latents,)),
        ],
        compiler_params=pltpu.CompilerParams(
            collective_id=0, has_side_effects=True, vmem_limit_bytes=32 << 20
        ),
    )(
        *(
            pltpu.with_memory_space_constraint(operand, pltpu.HBM)
            for operand in (
                video,
                jnp.swapaxes(first_weight, 3, 4).reshape(9, 3, part, channels),
                first_bias.reshape(1, part),
                second_weight.reshape(9, 3, channels, 2 * width),
                second_bias.reshape(1, width),
            )
        )
    )


def solution(mesh):
    placed = (
        P(("clip", "slab"), "tile", None, None),
        P(None, None, None, None, "chan"),
        P("chan"),
        P(),
        P("chan"),
    )
    return jax.shard_map(
        functools.partial(shards, mesh.shape["tile"], mesh.shape["slab"]),
        mesh=mesh,
        in_specs=placed,
        out_specs=P(("clip", "slab"), "tile", None, "chan"),
        check_vma=False,
    )
```

```python
import functools

import jax
import jax.numpy as jnp
from jax import lax
from jax.experimental import pallas as pl
from jax.experimental.pallas import tpu as pltpu
from jax.sharding import PartitionSpec as P

MESH = pl.DeviceIdType.MESH
BACK = 2


def kernel(
    tiles, slabs, video, w1, b1, w2, b2, out,
    v, h, k1, k2, bias1, bias2, pieces, incoming, going, going0, sum0, acc, acc2,
    load, w_s, b_s, z0_s, w1_r, b_r, a_r, z_r, f_r, q_r, o_r,
):
    x_s, p_s, o_s, q_s, z1_s = (load.at[n] for n in range(5))
    z_s = (z0_s, z1_s)
    frames, rows, columns, channels = video.shape
    half = rows // 2
    width = b2.shape[1]
    core = lax.axis_index("chan")
    tile = lax.axis_index("tile")
    slab = lax.axis_index("slab")
    other = 1 - core
    z_tile = tile + 2 * core - 1
    has_z = jnp.logical_and(z_tile >= 0, z_tile < tiles)
    no_z = jnp.logical_or(z_tile < 0, z_tile >= tiles)
    has_next = slab < slabs - 1
    no_next = slab == slabs - 1
    has_prev = slab > 0
    no_prev = slab == 0
    one = core == 1
    zero = core == 0
    above = tile > 0
    below = tile < tiles - 1
    peer = {"chan": other}
    z_minus = {"tile": tile - 1, "chan": 1}
    z_plus = {"tile": tile + 1, "chan": 0}
    next_same = {"slab": slab + 1}
    next_cross = {"slab": slab + 1, "chan": other}
    prev_same = {"slab": slab - 1}

    def both(*conditions):
        return functools.reduce(jnp.logical_and, conditions)

    def when(condition, body):
        if condition is None:
            body()
        else:
            pl.when(condition)(body)

    barrier = pltpu.get_barrier_semaphore()
    greetings = (
        (None, peer),
        (has_z, {"chan": other, "tile": z_tile}),
        (has_prev, {"slab": slab - 1, "chan": 1}),
        (both(one, has_prev, below), {"slab": slab - 1, "tile": tile + 1, "chan": 1}),
    )
    for condition, device in greetings:
        when(condition, lambda device=device: pl.semaphore_signal(
            barrier, inc=1, device_id=device, device_id_type=MESH))
    met = 1
    for condition, count in ((has_z, 1), (both(one, has_next), 2), (both(one, has_next, above), 1)):
        met = met + jnp.where(condition, count, 0)

    into_v = pltpu.make_async_copy(video, v.at[pl.ds(BACK, frames), pl.ds(half * other, rows)], load.at[0])
    own_w1 = pltpu.make_async_copy(w1, k1.at[:, :, core], load.at[1])
    own_b1 = pltpu.make_async_copy(b1, bias1.at[core], load.at[2])
    own_b2 = pltpu.make_async_copy(b2, bias2.at[0], load.at[4])
    own_w2 = [
        pltpu.make_async_copy(
            w2.at[:, :, :, pl.ds(pl.multiple_of(owner * width, width), width)], k2.at[n], load.at[3])
        for n, owner in enumerate((core, other))
    ]
    for copy in (into_v, own_w1, own_b1, own_b2):
        copy.start()

    def remote(src, dst, send, recv, device):
        return pltpu.make_async_remote_copy(
            src_ref=src, dst_ref=dst, send_sem=send, recv_sem=recv,
            device_id=device, device_id_type=MESH,
        )

    def wait_bytes(ref, semaphore):
        pltpu.make_async_copy(ref, ref, semaphore).wait()

    mine = pl.ds(half * core, half)
    theirs = pl.ds(half * other, half)
    halo_here = pl.ds(rows * core, half)
    frame0, frame1 = frames, frames + 1

    low, high = pl.ds(0, half), pl.ds(half, half)
    halo_low, halo_high = pl.ds(0, half), pl.ds(rows, half)

    def x_copies(device):
        return [
            [
                remote(v.at[frames + f, some], v.at[f, some], x_s, a_r.at[2 * f + n], device)
                for n, some in enumerate((low, high))
            ]
            for f in range(BACK)
        ]

    x_out = x_copies(next_same)
    x_in = x_copies(prev_same)
    slanted = remote(v.at[frames, low], v.at[0, halo_high], x_s, f_r.at[0], {"slab": slab + 1, **z_minus})
    forward_z = [
        [
            (above, remote(v.at[f, low], v.at[f, halo_high], z_s[0], f_r.at[f], z_minus)),
            (below, remote(v.at[f, high], v.at[f, halo_low], z_s[1], f_r.at[f], z_plus)),
        ]
        for f in range(BACK)
    ]
    f_in = [remote(v.at[f, low], v.at[f, halo_low], z_s[0], f_r.at[f], peer) for f in range(BACK)]
    forward_p = [remote(v.at[f, low], v.at[f, pl.ds(half, half)], p_s, a_r.at[f], peer) for f in range(BACK)]

    def share_h(index, count, place):
        return remote(
            h.at[pl.ds(index, count), low], h.at[pl.ds(index, count), pl.ds(half, half)], p_s, a_r.at[2 + place], peer
        )

    forward_h = [share_h(BACK, 1, 0), share_h(BACK + 1, 1, 1), share_h(frames, 2, 2), share_h(frames, 1, 2)]

    rest_h = [
        remote(
            h.at[pl.ds(BACK + n, n + 1), high], h.at[pl.ds(BACK + n, n + 1), pl.ds(rows, half)], o_s, a_r.at[n], peer
        )
        for n in range(2)
    ]

    def z_copies(count):
        some = pl.ds(BACK, count)
        return [
            [
                remote(video.at[pl.ds(0, count), pl.ds(n, 1)], v.at[some, pl.ds(rows + n, 1)], z_s[0], z_r.at[n], z_minus)
                for n in range(half)
            ],
            [
                remote(
                    v.at[some, pl.ds(rows - 1 - n, 1)], v.at[some, pl.ds(half - 1 - n, 1)], z_s[1], z_r.at[n], z_plus
                )
                for n in range(half)
            ],
        ]

    z_full = z_copies(frames)
    z_short = z_copies(frames - 1)

    def start_z(side):
        for condition, copies in ((has_next, z_full), (no_next, z_short)):

            @pl.when(condition)
            def _():
                for copy in copies[side]:
                    copy.start()

    to_peer = [
        remote(w1, k1.at[:, :, core], w_s, w1_r, peer),
        remote(b1, bias1.at[core], b_s.at[0], b_r.at[0], peer),
        remote(b2, bias2.at[1], b_s.at[1], b_r.at[1], peer),
    ]

    with jax.named_scope("entrybar"):
        pl.semaphore_wait(barrier, met)

    @pl.when(both(zero, above))
    def _():
        start_z(0)

    for copy in to_peer:
        copy.start()
    with jax.named_scope("loadwait"):
        into_v.wait()
        own_w1.wait()
        own_b1.wait()
        own_b2.wait()

    @pl.when(one)
    def _():
        @pl.when(has_next)
        def _():
            for f, n in ((1, 0), (1, 1), (0, 1), (0, 0)):
                x_out[f][n].start()

        @pl.when(below)
        def _():
            start_z(1)

    for copy in own_w2:
        copy.start()

    @pl.when(no_z)
    def _():
        v[:, halo_here] = jnp.zeros((v.shape[0], half, columns, channels), v.dtype)

    def taps(source, index, first, count, steps):
        return jnp.concatenate(
            [
                source[index + a, pl.ds(first + b, count)].reshape(count * columns, channels)
                for a in steps
                for b in range(3)
            ],
            axis=1,
        )

    def shifted(parts, size):
        column = lax.broadcasted_iota(jnp.int32, (parts.shape[0], size), 0) % columns
        before = pltpu.roll(parts[:, 0:size], 1, 0)
        after = pltpu.roll(parts[:, 2 * size : 3 * size], parts.shape[0] - 1, 0)
        total = parts[:, size : 2 * size] + jnp.where(column == 0, 0.0, before)
        return total + jnp.where(column == columns - 1, 0.0, after)

    def silu(total):
        return total / (1.0 + jnp.exp(-total))

    def hidden_sum(indices, first, count, steps):
        parts = lax.dot_general(
            jnp.concatenate([taps(v, index - 2, first, count, steps) for index in indices], axis=0),
            jnp.concatenate(
                [k1[3 * a + b].reshape(3 * channels, channels) for a in steps for b in range(3)], axis=1
            ),
            (((1,), (1,)), ((), ())),
            preferred_element_type=jnp.float32,
        )
        return shifted(parts, channels)

    no_rows = {"inner": (), "near": (), "far": (no_z,), "outer": (both(no_z, zero), both(no_z, one))}

    def hidden(kind, indices, first, count, oldest=0, newest=2, before=None):
        total = hidden_sum(indices, first, count, range(oldest, newest + 1))
        if before is not None:
            total = total + before
        bias = jnp.concatenate([bias1[0], bias1[1]], axis=1)
        value = silu(total + bias)
        value = value.reshape(len(indices), count, columns, channels)
        for n, index in enumerate(indices):
            new = value[n]
            if no_rows[kind]:
                new = jnp.stack([jnp.where(no_rows[kind][row], 0.0, new[row]) for row in range(count)])
            h[index, pl.ds(first, count)] = new.astype(h.dtype)

    def inner(*indices, oldest=0):
        with jax.named_scope("inner" + "_".join(map(str, indices))):
            hidden("inner", indices, half * other, half, oldest)

    def outer(*indices, oldest=0):
        with jax.named_scope("outer" + "_".join(map(str, indices))):
            hidden("outer", indices, half * core, half, oldest)

    def near(*indices, oldest=0):
        with jax.named_scope("near" + "_".join(map(str, indices))):
            hidden("near", indices, 1 + core, 1, oldest)

    def far(*indices, oldest=0):
        with jax.named_scope("far" + "_".join(map(str, indices))):
            hidden("far", indices, (rows - 1) * core, 1, oldest)

    def outer_begin(index):
        with jax.named_scope("outer%da" % index):
            acc2[...] = hidden_sum((index,), half * core, half, range(1, 3))

    def outer_end(index):
        with jax.named_scope("outer%db" % index):
            hidden("outer", (index,), half * core, half, 0, 0, acc2[...])

    def second(index, first, count, steps, blocks):
        matrix = jnp.concatenate(
            [
                jnp.concatenate([k2[n, 3 * (a + shift) + b, e] for n, shift in blocks for e in range(3)], axis=1)
                for a in steps
                for b in range(3)
            ],
            axis=0,
        )
        parts = jnp.dot(taps(h, index, first, count, steps), matrix, preferred_element_type=jnp.float32)
        return [shifted(parts[:, 3 * k * width : 3 * (k + 1) * width], width) for k in range(len(blocks))]

    whole = ((0, 0), (1, 0))

    def share(slot, local):
        place = half * core + local
        return [
            remote(pieces.at[slot, 0], incoming.at[place], q_s, q_r.at[slot], next_same),
            remote(pieces.at[slot, 1], incoming.at[place], q_s, q_r.at[slot], next_cross),
        ]

    shares = [share(0, other), share(1, core)]

    def send_share(slot, local):
        with jax.named_scope("share%d" % slot):
            halves = second(frames, local, 1, range(0, 2), whole)
            for n in (1, 0):
                pieces[slot, n] = halves[n].astype(pieces.dtype)
            for condition, order in ((zero, (0, 1)), (one, (1, 0))):

                @pl.when(condition)
                def _():
                    for n in order:
                        shares[slot][n].start()


    result = [
        remote(going.at[t - 1], out.at[t, mine], o_s, o_r.at[t], peer) for t in range(1, frames // 2)
    ]
    part0 = remote(going0, sum0.at[mine], o_s, o_r.at[0], peer)

    def latent(t):
        with jax.named_scope("latent%d" % t):
            own, away = second(2 * t, 0, half, range(3), whole)
            going[t - 1] = silu(away + bias2[1]).astype(out.dtype).reshape(half, columns, width)
            result[t - 1].start()
            out[t, mine] = silu(own + bias2[0]).astype(out.dtype).reshape(half, columns, width)

    def later_steps(steps=range(1, 3), start=True):
        with jax.named_scope("latent1a%d" % len(steps)):
            halves = second(2, 0, half, steps, whole)
            for n in range(2):
                acc[n] = halves[n] if start else acc[n] + halves[n]

    def own_steps(first):
        place = pl.ds(half * core if first == 0 else half, half)
        with jax.named_scope("own1a"):
            acc[0] = second(2, first, half, range(1, 3), ((0, 0),))[0]
        with jax.named_scope("own"):
            one_sum, then = second(2, first, half, range(0, 1), ((0, 2), (0, 0)))
            sum0[place] = one_sum.reshape(half, columns, width)
            out[1, place] = silu(then + acc[0] + bias2[0]).astype(out.dtype).reshape(half, columns, width)

    def last_steps():
        with jax.named_scope("tailA"):
            first, then = second(2, 0, half, range(0, 1), ((1, 2), (1, 0)))
            going0[...] = first.reshape(half, columns, width)
            part0.start()
            going[0] = silu(then + acc[1] + bias2[1]).astype(out.dtype).reshape(half, columns, width)
            result[0].start()
        with jax.named_scope("tailB"):
            first, then = second(2, 0, half, range(0, 1), ((0, 2), (0, 0)))
            sum0[mine] = first.reshape(half, columns, width)
            out[1, mine] = silu(then + acc[0] + bias2[0]).astype(out.dtype).reshape(half, columns, width)

    def wait_z(which, copies):
        with jax.named_scope("zwait%d" % which):

            @pl.when(has_z)
            def _():
                copies[0][which].wait_recv()

    def pass_on(f, n):
        with jax.named_scope("pass%d%d" % (f, n)):
            x_in[f][n].wait_recv()
            condition, copy = forward_z[f][n]
            if (f, n) != (0, 0):
                pl.when(condition)(copy.start)
            if n == 0:
                forward_p[f].start()

    def from_peer(name, copy):
        @pl.when(zero)
        def _():
            with jax.named_scope(name):
                copy.wait_recv()

    def halo_ready(name, copy):
        with jax.named_scope(name):

            @pl.when(has_z)
            def _():
                copy.wait_recv()

    def w2_ready():
        with jax.named_scope("w2wait"):
            wait_bytes(k2, load.at[3])

    with jax.named_scope("w1wait"):
        remote(w1, k1.at[:, :, other], w_s, w1_r, peer).wait_recv()
        remote(b1, bias1.at[other], b_s.at[0], b_r.at[0], peer).wait_recv()
        to_peer[2].wait_recv()

    last = frames + 1

    @pl.when(both(one, has_next))
    def _():
        inner(frames, last)
        forward_h[2].start()

    @pl.when(both(one, no_next))
    def _():
        inner(frames)
        forward_h[3].start()

    @pl.when(both(one, no_prev))
    def _():
        inner(3, oldest=1)
        forward_h[1].start()
        inner(2, oldest=2)
        forward_h[0].start()

    @pl.when(both(one, has_next, above))
    def _():
        slanted.start()

    @pl.when(has_next)
    def _():
        wait_z(0, z_full)
        near(frames, last)
        w2_ready()
        from_peer("hwait2", forward_h[2])
        send_share(0, other)

        wait_z(1, z_full)

        @pl.when(jnp.logical_or(above, has_prev))
        def _():
            far(frames, last)
            send_share(1, core)

    def middle():
        for index in range(frames - 1, 3, -1):
            inner(index)
            outer(index)
        for t in range(2, frames // 2):
            latent(t)

    def own_last():
        @pl.when(no_next)
        def _():
            wait_z(0, z_short)
            wait_z(1, z_short)
            outer(frames)

    def own_ready():
        @pl.when(no_next)
        def _():
            w2_ready()
            from_peer("hwait2", forward_h[3])

    @pl.when(no_prev)
    def _():
        own_last()
        own_ready()
        middle()

        @pl.when(both(has_next, tile == 0))
        def _():
            far(frames, last)
            outer(3, oldest=1)
            outer(2, oldest=2)

        @pl.when(jnp.logical_or(above, no_next))
        def _():
            outer(3, oldest=1)
            outer(2, oldest=2)

        @pl.when(one)
        def _():
            rest_h[1].start()
            rest_h[0].start()

        @pl.when(both(has_next, tile == 0))
        def _():
            send_share(1, core)

        @pl.when(one)
        def _():
            own_steps(0)

        @pl.when(zero)
        def _():
            forward_h[1].wait_recv()
            forward_h[0].wait_recv()
            later_steps()
            last_steps()
            for copy in rest_h:
                copy.wait_recv()
            own_steps(half)

    @pl.when(has_prev)
    def _():
        @pl.when(one)
        def _():
            pass_on(1, 0)
            pass_on(1, 1)
            inner(3)
            forward_h[1].start()
            pass_on(0, 1)
            own_last()
            pass_on(0, 0)
            inner(2)
            forward_h[0].start()

        @pl.when(zero)
        def _():
            own_last()

        own_ready()
        middle()
        later_steps(range(2, 3))
        @pl.when(one)
        def _():
            halo_ready("fwait1", f_in[1])
            halo_ready("fwait0", f_in[0])
            outer(3)
            outer(2)
            later_steps(range(1, 2), False)
            last_steps()

        @pl.when(zero)
        def _():
            forward_p[1].wait_recv()
            halo_ready("fwait1", f_in[1])
            forward_h[1].wait_recv()
            outer(3)
            later_steps(range(1, 2), False)
            outer_begin(2)
            forward_p[0].wait_recv()
            forward_h[0].wait_recv()
            halo_ready("fwait0", f_in[0])
            outer_end(2)
            last_steps()


    takes = jnp.logical_or(has_prev, one)

    @pl.when(takes)
    def _():
        remote(going0, sum0.at[theirs], o_s, o_r.at[0], peer).wait_recv()

    def close(first, count, extra):
        total = sum0[pl.ds(first, count)].reshape(count * columns, width)
        if extra:
            total = total + incoming[pl.ds(first, count)].reshape(count * columns, width).astype(jnp.float32)
        out[0, pl.ds(first, count)] = silu(total + bias2[0]).astype(out.dtype).reshape(count, columns, width)

    @pl.when(has_prev)
    def _():
        for slot, pair in enumerate(((half - 1, half), (0, rows - 1))):
            with jax.named_scope("close%d" % slot):
                wait_bytes(pieces.at[0], q_r.at[slot])
                for row in pair:
                    close(row, 1, True)

    @pl.when(no_prev)
    def _():
        close(0, rows, False)

    with jax.named_scope("ends"):
        for copy in to_peer:
            copy.wait_send()
        for t in range(1, frames // 2):
            copy = remote(going.at[t - 1], out.at[t, theirs], o_s, o_r.at[t], peer)
            when(takes if t == 1 else None, copy.wait_recv)
        wait_bytes(v.at[pl.ds(0, frames // 2 + 1), low], o_s)

        @pl.when(has_next)
        def _():
            wait_bytes(incoming, q_s)

        @pl.when(both(one, has_next, tile == 0))
        def _():
            wait_bytes(v.at[pl.ds(0, BACK), pl.ds(0, rows)], x_s)

        @pl.when(both(one, has_next, above))
        def _():
            wait_bytes(v.at[pl.ds(0, BACK), pl.ds(0, rows + 1)], x_s)

        for condition, count in (
            (both(no_prev, has_next), 4), (both(no_prev, no_next), 3),
            (both(has_prev, has_next), 6), (both(has_prev, no_next), 5),
        ):

            @pl.when(both(one, condition))
            def _():
                wait_bytes(v.at[pl.ds(0, count), low], p_s)

        for side, condition in ((0, above), (1, below)):
            forwards = both(one, condition)
            for after, count in ((has_next, frames), (no_next, frames - 1)):
                if side == 0:

                    @pl.when(both(zero, condition, after))
                    def _():
                        wait_bytes(v.at[pl.ds(0, count), low], z_s[0])

                else:

                    @pl.when(both(forwards, after, no_prev))
                    def _():
                        wait_bytes(v.at[pl.ds(0, count), low], z_s[1])

                    @pl.when(both(forwards, after, has_prev))
                    def _():
                        wait_bytes(v.at[pl.ds(0, count + BACK), low], z_s[1])

            if side == 0:

                @pl.when(both(forwards, has_prev))
                def _():
                    wait_bytes(v.at[pl.ds(0, 1), low], z_s[0])


def shards(tiles, slabs, video, first_weight, first_bias, second_weight, second_bias):
    frames, rows, columns, channels = video.shape
    half = rows // 2
    assert half == 2 and first_weight.shape[3] == channels == second_bias.shape[0] and frames >= 4 and frames % 2 == 0
    part = first_bias.shape[0]
    width = second_bias.shape[0]
    anywhere = pl.BlockSpec(memory_space=pltpu.HBM)
    inside = pl.BlockSpec(memory_space=pltpu.VMEM)
    dma = pltpu.SemaphoreType.DMA
    vmem = pltpu.VMEM
    latents = frames // 2
    return pl.pallas_call(
        functools.partial(kernel, tiles, slabs),
        out_shape=jax.ShapeDtypeStruct((latents, rows, columns, width), jnp.bfloat16),
        in_specs=[anywhere] * 5,
        out_specs=inside,
        scratch_shapes=[
            vmem((BACK + frames, rows + 2, columns, channels), jnp.bfloat16),
            vmem((frames + 2, half + 4, columns, channels), jnp.bfloat16),
            vmem((9, 3, 2, part, channels), jnp.bfloat16),
            vmem((2, 9, 3, channels, width), jnp.bfloat16),
            vmem((2, 1, part), jnp.float32),
            vmem((2, 1, width), jnp.float32),
            vmem((2, 2, columns, width), jnp.bfloat16),
            vmem((rows, columns, width), jnp.bfloat16),
            vmem((latents - 1, half, columns, width), jnp.bfloat16),
            vmem((half, columns, width), jnp.float32),
            vmem((rows, columns, width), jnp.float32),
            vmem((2, half * columns, width), jnp.float32),
            vmem((half * columns, channels), jnp.float32),
            dma((5,)), dma, dma((2,)), dma, dma, dma((2,)), dma((2 * BACK + 1,)), dma((2,)), dma((BACK,)), dma((2,)),
            dma((latents,)),
        ],
        compiler_params=pltpu.CompilerParams(
            collective_id=0, has_side_effects=True, vmem_limit_bytes=32 << 20
        ),
    )(
        *(
            pltpu.with_memory_space_constraint(operand, pltpu.HBM)
            for operand in (
                video,
                jnp.swapaxes(first_weight, 3, 4).reshape(9, 3, part, channels),
                first_bias.reshape(1, part),
                second_weight.reshape(9, 3, channels, 2 * width),
                second_bias.reshape(1, width),
            )
        )
    )


def solution(mesh):
    placed = (
        P(("clip", "slab"), "tile", None, None),
        P(None, None, None, None, "chan"),
        P("chan"),
        P(),
        P("chan"),
    )
    return jax.shard_map(
        functools.partial(shards, mesh.shape["tile"], mesh.shape["slab"]),
        mesh=mesh,
        in_specs=placed,
        out_specs=P(("clip", "slab"), "tile", None, "chan"),
        check_vma=False,
    )
```

```python
import functools

import jax
import jax.numpy as jnp
from jax import lax
from jax.experimental import pallas as pl
from jax.experimental.pallas import tpu as pltpu
from jax.sharding import PartitionSpec as P

MESH = pl.DeviceIdType.MESH
BACK = 2


def kernel(
    tiles, slabs, video, w1, b1, w2, b2, out,
    v, h, k1, k2, bias1, bias2, pieces, incoming, going, going0, sum0, acc, acc2,
    load, w_s, b_s, z0_s, w1_r, b_r, a_r, z_r, f_r, q_r, o_r,
):
    x_s, p_s, o_s, q_s, z1_s = (load.at[n] for n in range(5))
    z_s = (z0_s, z1_s)
    frames, rows, columns, channels = video.shape
    half = rows // 2
    width = b2.shape[1]
    core = lax.axis_index("chan")
    tile = lax.axis_index("tile")
    slab = lax.axis_index("slab")
    other = 1 - core
    z_tile = tile + 2 * core - 1
    has_z = jnp.logical_and(z_tile >= 0, z_tile < tiles)
    no_z = jnp.logical_or(z_tile < 0, z_tile >= tiles)
    has_next = slab < slabs - 1
    no_next = slab == slabs - 1
    has_prev = slab > 0
    no_prev = slab == 0
    one = core == 1
    zero = core == 0
    above = tile > 0
    below = tile < tiles - 1
    peer = {"chan": other}
    z_minus = {"tile": tile - 1, "chan": 1}
    z_plus = {"tile": tile + 1, "chan": 0}
    next_same = {"slab": slab + 1}
    next_cross = {"slab": slab + 1, "chan": other}
    prev_same = {"slab": slab - 1}

    def both(*conditions):
        return functools.reduce(jnp.logical_and, conditions)

    def when(condition, body):
        if condition is None:
            body()
        else:
            pl.when(condition)(body)

    barrier = pltpu.get_barrier_semaphore()
    greetings = (
        (None, peer),
        (has_z, {"chan": other, "tile": z_tile}),
        (has_prev, {"slab": slab - 1, "chan": 1}),
        (both(one, has_prev, below), {"slab": slab - 1, "tile": tile + 1, "chan": 1}),
    )
    for condition, device in greetings:
        when(condition, lambda device=device: pl.semaphore_signal(
            barrier, inc=1, device_id=device, device_id_type=MESH))
    met = 1
    for condition, count in ((has_z, 1), (both(one, has_next), 2), (both(one, has_next, above), 1)):
        met = met + jnp.where(condition, count, 0)

    into_v = pltpu.make_async_copy(video, v.at[pl.ds(BACK, frames), pl.ds(half * other, rows)], load.at[0])
    own_w1 = pltpu.make_async_copy(w1, k1.at[:, :, core], load.at[1])
    own_b1 = pltpu.make_async_copy(b1, bias1.at[core], load.at[2])
    own_b2 = pltpu.make_async_copy(b2, bias2.at[0], load.at[4])
    own_w2 = [
        pltpu.make_async_copy(
            w2.at[:, :, :, pl.ds(pl.multiple_of(owner * width, width), width)], k2.at[n], load.at[3])
        for n, owner in enumerate((core, other))
    ]
    for copy in (into_v, own_w1, own_b1, own_b2):
        copy.start()

    def remote(src, dst, send, recv, device):
        return pltpu.make_async_remote_copy(
            src_ref=src, dst_ref=dst, send_sem=send, recv_sem=recv,
            device_id=device, device_id_type=MESH,
        )

    def wait_bytes(ref, semaphore):
        pltpu.make_async_copy(ref, ref, semaphore).wait()

    mine = pl.ds(half * core, half)
    theirs = pl.ds(half * other, half)
    halo_here = pl.ds(rows * core, half)
    frame0, frame1 = frames, frames + 1

    low, high = pl.ds(0, half), pl.ds(half, half)
    halo_low, halo_high = pl.ds(0, half), pl.ds(rows, half)

    def x_copies(device):
        return [
            [
                remote(v.at[frames + f, some], v.at[f, some], x_s, a_r.at[2 * f + n], device)
                for n, some in enumerate((low, high))
            ]
            for f in range(BACK)
        ]

    x_out = x_copies(next_same)
    x_in = x_copies(prev_same)
    slanted = remote(v.at[frames, low], v.at[0, halo_high], x_s, f_r.at[0], {"slab": slab + 1, **z_minus})
    forward_z = [
        [
            (above, remote(v.at[f, low], v.at[f, halo_high], z_s[0], f_r.at[f], z_minus)),
            (below, remote(v.at[f, high], v.at[f, halo_low], z_s[1], f_r.at[f], z_plus)),
        ]
        for f in range(BACK)
    ]
    f_in = [remote(v.at[f, low], v.at[f, halo_low], z_s[0], f_r.at[f], peer) for f in range(BACK)]
    forward_p = [remote(v.at[f, low], v.at[f, pl.ds(half, half)], p_s, a_r.at[f], peer) for f in range(BACK)]

    def share_h(index, count, place):
        return remote(
            h.at[pl.ds(index, count), low], h.at[pl.ds(index, count), pl.ds(half, half)], p_s, a_r.at[2 + place], peer
        )

    forward_h = [share_h(BACK, 1, 0), share_h(BACK + 1, 1, 1), share_h(frames, 2, 2), share_h(frames, 1, 2)]

    rest_h = [
        remote(
            h.at[pl.ds(BACK + n, n + 1), high], h.at[pl.ds(BACK + n, n + 1), pl.ds(rows, half)], o_s, a_r.at[n], peer
        )
        for n in range(2)
    ]

    def z_copies(count):
        some = pl.ds(BACK, count)
        return [
            [
                remote(video.at[pl.ds(0, count), pl.ds(n, 1)], v.at[some, pl.ds(rows + n, 1)], z_s[0], z_r.at[n], z_minus)
                for n in range(half)
            ],
            [
                remote(
                    v.at[some, pl.ds(rows - 1 - n, 1)], v.at[some, pl.ds(half - 1 - n, 1)], z_s[1], z_r.at[n], z_plus
                )
                for n in range(half)
            ],
        ]

    z_full = z_copies(frames)
    z_short = z_copies(frames - 1)

    def start_z(side):
        for condition, copies in ((has_next, z_full), (no_next, z_short)):

            @pl.when(condition)
            def _():
                for copy in copies[side]:
                    copy.start()

    to_peer = [
        remote(w1, k1.at[:, :, core], w_s, w1_r, peer),
        remote(b1, bias1.at[core], b_s.at[0], b_r.at[0], peer),
        remote(b2, bias2.at[1], b_s.at[1], b_r.at[1], peer),
    ]

    with jax.named_scope("entrybar"):
        pl.semaphore_wait(barrier, met)

    @pl.when(both(zero, above))
    def _():
        start_z(0)

    for copy in to_peer:
        copy.start()
    with jax.named_scope("loadwait"):
        into_v.wait()
        own_w1.wait()
        own_b1.wait()
        own_b2.wait()

    @pl.when(one)
    def _():
        @pl.when(has_next)
        def _():
            for f, n in ((1, 0), (1, 1), (0, 1), (0, 0)):
                x_out[f][n].start()

        @pl.when(below)
        def _():
            start_z(1)

    for copy in own_w2:
        copy.start()

    @pl.when(no_z)
    def _():
        v[:, halo_here] = jnp.zeros((v.shape[0], half, columns, channels), v.dtype)

    def taps(source, index, first, count, steps):
        return jnp.concatenate(
            [
                source[index + a, pl.ds(first + b, count)].reshape(count * columns, channels)
                for a in steps
                for b in range(3)
            ],
            axis=1,
        )

    def shifted(parts, size):
        column = lax.broadcasted_iota(jnp.int32, (parts.shape[0], size), 0) % columns
        before = pltpu.roll(parts[:, 0:size], 1, 0)
        after = pltpu.roll(parts[:, 2 * size : 3 * size], parts.shape[0] - 1, 0)
        total = parts[:, size : 2 * size] + jnp.where(column == 0, 0.0, before)
        return total + jnp.where(column == columns - 1, 0.0, after)

    def silu(total):
        return total / (1.0 + jnp.exp(-total))

    def hidden_sum(indices, first, count, steps):
        parts = lax.dot_general(
            jnp.concatenate([taps(v, index - 2, first, count, steps) for index in indices], axis=0),
            jnp.concatenate(
                [k1[3 * a + b].reshape(3 * channels, channels) for a in steps for b in range(3)], axis=1
            ),
            (((1,), (1,)), ((), ())),
            preferred_element_type=jnp.float32,
        )
        return shifted(parts, channels)

    no_rows = {"inner": (), "near": (), "far": (no_z,), "outer": (both(no_z, zero), both(no_z, one))}

    def hidden(kind, indices, first, count, oldest=0, newest=2, before=None):
        total = hidden_sum(indices, first, count, range(oldest, newest + 1))
        if before is not None:
            total = total + before
        bias = jnp.concatenate([bias1[0], bias1[1]], axis=1)
        value = silu(total + bias)
        value = value.reshape(len(indices), count, columns, channels)
        for n, index in enumerate(indices):
            new = value[n]
            if no_rows[kind]:
                new = jnp.stack([jnp.where(no_rows[kind][row], 0.0, new[row]) for row in range(count)])
            h[index, pl.ds(first, count)] = new.astype(h.dtype)

    def inner(*indices, oldest=0):
        with jax.named_scope("inner" + "_".join(map(str, indices))):
            hidden("inner", indices, half * other, half, oldest)

    def outer(*indices, oldest=0):
        with jax.named_scope("outer" + "_".join(map(str, indices))):
            hidden("outer", indices, half * core, half, oldest)

    def near(*indices, oldest=0):
        with jax.named_scope("near" + "_".join(map(str, indices))):
            hidden("near", indices, 1 + core, 1, oldest)

    def far(*indices, oldest=0):
        with jax.named_scope("far" + "_".join(map(str, indices))):
            hidden("far", indices, (rows - 1) * core, 1, oldest)

    def outer_begin(index):
        with jax.named_scope("outer%da" % index):
            acc2[...] = hidden_sum((index,), half * core, half, range(1, 3))

    def outer_end(index):
        with jax.named_scope("outer%db" % index):
            hidden("outer", (index,), half * core, half, 0, 0, acc2[...])

    def second(index, first, count, steps, blocks):
        matrix = jnp.concatenate(
            [
                jnp.concatenate([k2[n, 3 * (a + shift) + b, e] for n, shift in blocks for e in range(3)], axis=1)
                for a in steps
                for b in range(3)
            ],
            axis=0,
        )
        parts = jnp.dot(taps(h, index, first, count, steps), matrix, preferred_element_type=jnp.float32)
        return [shifted(parts[:, 3 * k * width : 3 * (k + 1) * width], width) for k in range(len(blocks))]

    whole = ((0, 0), (1, 0))

    def share(slot, local):
        place = half * core + local
        return [
            remote(pieces.at[slot, 0], incoming.at[place], q_s, q_r.at[slot], next_same),
            remote(pieces.at[slot, 1], incoming.at[place], q_s, q_r.at[slot], next_cross),
        ]

    shares = [share(0, other), share(1, core)]

    def send_share(slot, local):
        with jax.named_scope("share%d" % slot):
            halves = second(frames, local, 1, range(0, 2), whole)
            for n in (1, 0):
                pieces[slot, n] = halves[n].astype(pieces.dtype)
            for condition, order in ((zero, (0, 1)), (one, (1, 0))):

                @pl.when(condition)
                def _():
                    for n in order:
                        shares[slot][n].start()


    result = [
        remote(going.at[t - 1], out.at[t, mine], o_s, o_r.at[t], peer) for t in range(1, frames // 2)
    ]
    part0 = remote(going0, sum0.at[mine], o_s, o_r.at[0], peer)

    def latent(t):
        with jax.named_scope("latent%d" % t):
            own, away = second(2 * t, 0, half, range(3), whole)
            going[t - 1] = silu(away + bias2[1]).astype(out.dtype).reshape(half, columns, width)
            result[t - 1].start()
            out[t, mine] = silu(own + bias2[0]).astype(out.dtype).reshape(half, columns, width)

    def later_steps(steps=range(1, 3), start=True):
        with jax.named_scope("latent1a%d" % len(steps)):
            halves = second(2, 0, half, steps, whole)
            for n in range(2):
                acc[n] = halves[n] if start else acc[n] + halves[n]

    def own_steps(first):
        place = pl.ds(half * core if first == 0 else half, half)
        with jax.named_scope("own1a"):
            acc[0] = second(2, first, half, range(1, 3), ((0, 0),))[0]
        with jax.named_scope("own"):
            one_sum, then = second(2, first, half, range(0, 1), ((0, 2), (0, 0)))
            sum0[place] = one_sum.reshape(half, columns, width)
            out[1, place] = silu(then + acc[0] + bias2[0]).astype(out.dtype).reshape(half, columns, width)

    def last_steps():
        with jax.named_scope("tailA"):
            first, then = second(2, 0, half, range(0, 1), ((1, 2), (1, 0)))
            going0[...] = first.reshape(half, columns, width)
            part0.start()
            going[0] = silu(then + acc[1] + bias2[1]).astype(out.dtype).reshape(half, columns, width)
            result[0].start()
        with jax.named_scope("tailB"):
            first, then = second(2, 0, half, range(0, 1), ((0, 2), (0, 0)))
            sum0[mine] = first.reshape(half, columns, width)
            out[1, mine] = silu(then + acc[0] + bias2[0]).astype(out.dtype).reshape(half, columns, width)

    def wait_z(which, copies):
        with jax.named_scope("zwait%d" % which):

            @pl.when(has_z)
            def _():
                copies[0][which].wait_recv()

    def pass_on(f, n):
        with jax.named_scope("pass%d%d" % (f, n)):
            x_in[f][n].wait_recv()
            condition, copy = forward_z[f][n]
            if (f, n) != (0, 0):
                pl.when(condition)(copy.start)
            if n == 0:
                forward_p[f].start()

    def from_peer(name, copy):
        @pl.when(zero)
        def _():
            with jax.named_scope(name):
                copy.wait_recv()

    def halo_ready(name, copy):
        with jax.named_scope(name):

            @pl.when(has_z)
            def _():
                copy.wait_recv()

    def w2_ready():
        with jax.named_scope("w2wait"):
            wait_bytes(k2, load.at[3])

    with jax.named_scope("w1wait"):
        remote(w1, k1.at[:, :, other], w_s, w1_r, peer).wait_recv()
        remote(b1, bias1.at[other], b_s.at[0], b_r.at[0], peer).wait_recv()
        to_peer[2].wait_recv()

    last = frames + 1

    @pl.when(both(one, has_next))
    def _():
        inner(frames, last)
        forward_h[2].start()

    @pl.when(both(one, no_next))
    def _():
        inner(frames)
        forward_h[3].start()

    @pl.when(both(one, no_prev))
    def _():
        inner(3, oldest=1)
        forward_h[1].start()
        inner(2, oldest=2)
        forward_h[0].start()

    @pl.when(both(one, has_next, above))
    def _():
        slanted.start()

    @pl.when(has_next)
    def _():
        wait_z(0, z_full)
        near(frames, last)
        w2_ready()
        from_peer("hwait2", forward_h[2])
        send_share(0, other)

        wait_z(1, z_full)

        @pl.when(jnp.logical_or(above, has_prev))
        def _():
            far(frames, last)
            send_share(1, core)

    def middle():
        for index in range(frames - 1, 3, -1):
            inner(index)
            outer(index)
        for t in range(2, frames // 2):
            latent(t)

    def own_last():
        @pl.when(no_next)
        def _():
            wait_z(0, z_short)
            wait_z(1, z_short)
            outer(frames)

    def own_ready():
        @pl.when(no_next)
        def _():
            w2_ready()
            from_peer("hwait2", forward_h[3])

    @pl.when(no_prev)
    def _():
        own_last()
        own_ready()
        middle()

        @pl.when(both(has_next, tile == 0))
        def _():
            far(frames, last)
            outer(3, oldest=1)
            outer(2, oldest=2)

        @pl.when(jnp.logical_or(above, no_next))
        def _():
            outer(3, oldest=1)
            outer(2, oldest=2)

        @pl.when(one)
        def _():
            rest_h[1].start()
            rest_h[0].start()

        @pl.when(both(has_next, tile == 0))
        def _():
            send_share(1, core)

        @pl.when(one)
        def _():
            own_steps(0)

        @pl.when(zero)
        def _():
            forward_h[1].wait_recv()
            forward_h[0].wait_recv()
            later_steps()
            last_steps()
            for copy in rest_h:
                copy.wait_recv()
            own_steps(half)

    @pl.when(has_prev)
    def _():
        @pl.when(one)
        def _():
            pass_on(1, 0)
            pass_on(1, 1)
            inner(3)
            forward_h[1].start()
            pass_on(0, 1)
            own_last()
            pass_on(0, 0)
            inner(2)
            forward_h[0].start()

        @pl.when(zero)
        def _():
            own_last()

        own_ready()
        middle()
        later_steps(range(2, 3))
        @pl.when(one)
        def _():
            halo_ready("fwait1", f_in[1])
            halo_ready("fwait0", f_in[0])
            outer(3)
            outer(2)
            later_steps(range(1, 2), False)
            last_steps()

        @pl.when(zero)
        def _():
            forward_p[1].wait_recv()
            halo_ready("fwait1", f_in[1])
            outer(3)
            forward_h[1].wait_recv()
            forward_p[0].wait_recv()
            forward_h[0].wait_recv()
            halo_ready("fwait0", f_in[0])
            outer(2)
            later_steps(range(1, 2), False)
            last_steps()


    takes = jnp.logical_or(has_prev, one)

    @pl.when(takes)
    def _():
        remote(going0, sum0.at[theirs], o_s, o_r.at[0], peer).wait_recv()

    def close(first, count, extra):
        total = sum0[pl.ds(first, count)].reshape(count * columns, width)
        if extra:
            total = total + incoming[pl.ds(first, count)].reshape(count * columns, width).astype(jnp.float32)
        out[0, pl.ds(first, count)] = silu(total + bias2[0]).astype(out.dtype).reshape(count, columns, width)

    @pl.when(has_prev)
    def _():
        for slot, pair in enumerate(((half - 1, half), (0, rows - 1))):
            with jax.named_scope("close%d" % slot):
                wait_bytes(pieces.at[0], q_r.at[slot])
                for row in pair:
                    close(row, 1, True)

    @pl.when(no_prev)
    def _():
        close(0, rows, False)

    with jax.named_scope("ends"):
        for copy in to_peer:
            copy.wait_send()
        for t in range(1, frames // 2):
            copy = remote(going.at[t - 1], out.at[t, theirs], o_s, o_r.at[t], peer)
            when(takes if t == 1 else None, copy.wait_recv)
        wait_bytes(v.at[pl.ds(0, frames // 2 + 1), low], o_s)

        @pl.when(has_next)
        def _():
            wait_bytes(incoming, q_s)

        @pl.when(both(one, has_next, tile == 0))
        def _():
            wait_bytes(v.at[pl.ds(0, BACK), pl.ds(0, rows)], x_s)

        @pl.when(both(one, has_next, above))
        def _():
            wait_bytes(v.at[pl.ds(0, BACK), pl.ds(0, rows + 1)], x_s)

        for condition, count in (
            (both(no_prev, has_next), 4), (both(no_prev, no_next), 3),
            (both(has_prev, has_next), 6), (both(has_prev, no_next), 5),
        ):

            @pl.when(both(one, condition))
            def _():
                wait_bytes(v.at[pl.ds(0, count), low], p_s)

        for side, condition in ((0, above), (1, below)):
            forwards = both(one, condition)
            for after, count in ((has_next, frames), (no_next, frames - 1)):
                if side == 0:

                    @pl.when(both(zero, condition, after))
                    def _():
                        wait_bytes(v.at[pl.ds(0, count), low], z_s[0])

                else:

                    @pl.when(both(forwards, after, no_prev))
                    def _():
                        wait_bytes(v.at[pl.ds(0, count), low], z_s[1])

                    @pl.when(both(forwards, after, has_prev))
                    def _():
                        wait_bytes(v.at[pl.ds(0, count + BACK), low], z_s[1])

            if side == 0:

                @pl.when(both(forwards, has_prev))
                def _():
                    wait_bytes(v.at[pl.ds(0, 1), low], z_s[0])


def shards(tiles, slabs, video, first_weight, first_bias, second_weight, second_bias):
    frames, rows, columns, channels = video.shape
    half = rows // 2
    assert half == 2 and first_weight.shape[3] == channels == second_bias.shape[0] and frames >= 4 and frames % 2 == 0
    part = first_bias.shape[0]
    width = second_bias.shape[0]
    anywhere = pl.BlockSpec(memory_space=pltpu.HBM)
    inside = pl.BlockSpec(memory_space=pltpu.VMEM)
    dma = pltpu.SemaphoreType.DMA
    vmem = pltpu.VMEM
    latents = frames // 2
    return pl.pallas_call(
        functools.partial(kernel, tiles, slabs),
        out_shape=jax.ShapeDtypeStruct((latents, rows, columns, width), jnp.bfloat16),
        in_specs=[anywhere] * 5,
        out_specs=inside,
        scratch_shapes=[
            vmem((BACK + frames, rows + 2, columns, channels), jnp.bfloat16),
            vmem((frames + 2, half + 4, columns, channels), jnp.bfloat16),
            vmem((9, 3, 2, part, channels), jnp.bfloat16),
            vmem((2, 9, 3, channels, width), jnp.bfloat16),
            vmem((2, 1, part), jnp.float32),
            vmem((2, 1, width), jnp.float32),
            vmem((2, 2, columns, width), jnp.bfloat16),
            vmem((rows, columns, width), jnp.bfloat16),
            vmem((latents - 1, half, columns, width), jnp.bfloat16),
            vmem((half, columns, width), jnp.float32),
            vmem((rows, columns, width), jnp.float32),
            vmem((2, half * columns, width), jnp.float32),
            vmem((half * columns, channels), jnp.float32),
            dma((5,)), dma, dma((2,)), dma, dma, dma((2,)), dma((2 * BACK + 1,)), dma((2,)), dma((BACK,)), dma((2,)),
            dma((latents,)),
        ],
        compiler_params=pltpu.CompilerParams(
            collective_id=0, has_side_effects=True, vmem_limit_bytes=32 << 20
        ),
    )(
        *(
            pltpu.with_memory_space_constraint(operand, pltpu.HBM)
            for operand in (
                video,
                jnp.swapaxes(first_weight, 3, 4).reshape(9, 3, part, channels),
                first_bias.reshape(1, part),
                second_weight.reshape(9, 3, channels, 2 * width),
                second_bias.reshape(1, width),
            )
        )
    )


def solution(mesh):
    placed = (
        P(("clip", "slab"), "tile", None, None),
        P(None, None, None, None, "chan"),
        P("chan"),
        P(),
        P("chan"),
    )
    return jax.shard_map(
        functools.partial(shards, mesh.shape["tile"], mesh.shape["slab"]),
        mesh=mesh,
        in_specs=placed,
        out_specs=P(("clip", "slab"), "tile", None, "chan"),
        check_vma=False,
    )
```

```python
import functools

import jax
import jax.numpy as jnp
from jax import lax
from jax.experimental import pallas as pl
from jax.experimental.pallas import tpu as pltpu
from jax.sharding import PartitionSpec as P

MESH = pl.DeviceIdType.MESH
BACK = 2


def kernel(
    tiles, slabs, video, w1, b1, w2, b2, out,
    v, h, k1, k2, bias1, bias2, pieces, incoming, going, going0, sum0, acc, acc2,
    load, w_s, b_s, z0_s, w1_r, b_r, a_r, z_r, f_r, q_r, o_r,
):
    x_s, p_s, o_s, q_s, z1_s = (load.at[n] for n in range(5))
    z_s = (z0_s, z1_s)
    frames, rows, columns, channels = video.shape
    half = rows // 2
    width = b2.shape[1]
    core = lax.axis_index("chan")
    tile = lax.axis_index("tile")
    slab = lax.axis_index("slab")
    other = 1 - core
    z_tile = tile + 2 * core - 1
    has_z = jnp.logical_and(z_tile >= 0, z_tile < tiles)
    no_z = jnp.logical_or(z_tile < 0, z_tile >= tiles)
    has_next = slab < slabs - 1
    no_next = slab == slabs - 1
    has_prev = slab > 0
    no_prev = slab == 0
    one = core == 1
    zero = core == 0
    above = tile > 0
    below = tile < tiles - 1
    peer = {"chan": other}
    z_minus = {"tile": tile - 1, "chan": 1}
    z_plus = {"tile": tile + 1, "chan": 0}
    next_same = {"slab": slab + 1}
    next_cross = {"slab": slab + 1, "chan": other}
    prev_same = {"slab": slab - 1}

    def both(*conditions):
        return functools.reduce(jnp.logical_and, conditions)

    def when(condition, body):
        if condition is None:
            body()
        else:
            pl.when(condition)(body)

    barrier = pltpu.get_barrier_semaphore()
    greetings = (
        (None, peer),
        (has_z, {"chan": other, "tile": z_tile}),
        (has_prev, {"slab": slab - 1, "chan": 1}),
        (both(one, has_prev, below), {"slab": slab - 1, "tile": tile + 1, "chan": 1}),
    )
    for condition, device in greetings:
        when(condition, lambda device=device: pl.semaphore_signal(
            barrier, inc=1, device_id=device, device_id_type=MESH))
    met = 1
    for condition, count in ((has_z, 1), (both(one, has_next), 2), (both(one, has_next, above), 1)):
        met = met + jnp.where(condition, count, 0)

    into_v = pltpu.make_async_copy(video, v.at[pl.ds(BACK, frames), pl.ds(half * other, rows)], load.at[0])
    own_w1 = pltpu.make_async_copy(w1, k1.at[:, :, core], load.at[1])
    own_b1 = pltpu.make_async_copy(b1, bias1.at[core], load.at[2])
    own_b2 = pltpu.make_async_copy(b2, bias2.at[0], load.at[4])
    own_w2 = [
        pltpu.make_async_copy(
            w2.at[:, :, :, pl.ds(pl.multiple_of(owner * width, width), width)], k2.at[n], load.at[3])
        for n, owner in enumerate((core, other))
    ]
    for copy in (into_v, own_w1, own_b1, own_b2):
        copy.start()

    def remote(src, dst, send, recv, device):
        return pltpu.make_async_remote_copy(
            src_ref=src, dst_ref=dst, send_sem=send, recv_sem=recv,
            device_id=device, device_id_type=MESH,
        )

    def wait_bytes(ref, semaphore):
        pltpu.make_async_copy(ref, ref, semaphore).wait()

    mine = pl.ds(half * core, half)
    theirs = pl.ds(half * other, half)
    halo_here = pl.ds(rows * core, half)
    frame0, frame1 = frames, frames + 1

    low, high = pl.ds(0, half), pl.ds(half, half)
    halo_low, halo_high = pl.ds(0, half), pl.ds(rows, half)

    def x_copies(device):
        return [
            [
                remote(v.at[frames + f, some], v.at[f, some], x_s, a_r.at[2 * f + n], device)
                for n, some in enumerate((low, high))
            ]
            for f in range(BACK)
        ]

    x_out = x_copies(next_same)
    x_in = x_copies(prev_same)
    slanted = remote(v.at[frames, low], v.at[0, halo_high], x_s, f_r.at[0], {"slab": slab + 1, **z_minus})
    forward_z = [
        [
            (above, remote(v.at[f, low], v.at[f, halo_high], z_s[0], f_r.at[f], z_minus)),
            (below, remote(v.at[f, high], v.at[f, halo_low], z_s[1], f_r.at[f], z_plus)),
        ]
        for f in range(BACK)
    ]
    f_in = [remote(v.at[f, low], v.at[f, halo_low], z_s[0], f_r.at[f], peer) for f in range(BACK)]
    forward_p = [remote(v.at[f, low], v.at[f, pl.ds(half, half)], p_s, a_r.at[f], peer) for f in range(BACK)]

    def share_h(index, count, place):
        return remote(
            h.at[pl.ds(index, count), low], h.at[pl.ds(index, count), pl.ds(half, half)], p_s, a_r.at[2 + place], peer
        )

    forward_h = [share_h(BACK, 1, 0), share_h(BACK + 1, 1, 1), share_h(frames, 2, 2), share_h(frames, 1, 2)]

    rest_h = [
        remote(
            h.at[pl.ds(BACK + n, n + 1), high], h.at[pl.ds(BACK + n, n + 1), pl.ds(rows, half)], o_s, a_r.at[n], peer
        )
        for n in range(2)
    ]

    def z_copies(count):
        some = pl.ds(BACK, count)
        return [
            [
                remote(video.at[pl.ds(0, count), pl.ds(n, 1)], v.at[some, pl.ds(rows + n, 1)], z_s[0], z_r.at[n], z_minus)
                for n in range(half)
            ],
            [
                remote(
                    v.at[some, pl.ds(rows - 1 - n, 1)], v.at[some, pl.ds(half - 1 - n, 1)], z_s[1], z_r.at[n], z_plus
                )
                for n in range(half)
            ],
        ]

    z_full = z_copies(frames)
    z_short = z_copies(frames - 1)

    def start_z(side):
        for condition, copies in ((has_next, z_full), (no_next, z_short)):

            @pl.when(condition)
            def _():
                for copy in copies[side]:
                    copy.start()

    to_peer = [
        remote(w1, k1.at[:, :, core], w_s, w1_r, peer),
        remote(b1, bias1.at[core], b_s.at[0], b_r.at[0], peer),
        remote(b2, bias2.at[1], b_s.at[1], b_r.at[1], peer),
    ]

    with jax.named_scope("entrybar"):
        pl.semaphore_wait(barrier, met)

    @pl.when(both(zero, above))
    def _():
        start_z(0)

    for copy in to_peer:
        copy.start()
    with jax.named_scope("loadwait"):
        into_v.wait()
        own_w1.wait()
        own_b1.wait()
        own_b2.wait()

    @pl.when(one)
    def _():
        @pl.when(has_next)
        def _():
            for f, n in ((1, 0), (1, 1), (0, 1), (0, 0)):
                x_out[f][n].start()

        @pl.when(below)
        def _():
            start_z(1)

    for copy in own_w2:
        copy.start()

    @pl.when(no_z)
    def _():
        v[:, halo_here] = jnp.zeros((v.shape[0], half, columns, channels), v.dtype)

    def taps(source, index, first, count, steps):
        return jnp.concatenate(
            [
                source[index + a, pl.ds(first + b, count)].reshape(count * columns, channels)
                for a in steps
                for b in range(3)
            ],
            axis=1,
        )

    def shifted(parts, size):
        column = lax.broadcasted_iota(jnp.int32, (parts.shape[0], size), 0) % columns
        before = pltpu.roll(parts[:, 0:size], 1, 0)
        after = pltpu.roll(parts[:, 2 * size : 3 * size], parts.shape[0] - 1, 0)
        total = parts[:, size : 2 * size] + jnp.where(column == 0, 0.0, before)
        return total + jnp.where(column == columns - 1, 0.0, after)

    def silu(total):
        return total / (1.0 + jnp.exp(-total))

    def hidden_sum(indices, first, count, steps):
        parts = lax.dot_general(
            jnp.concatenate([taps(v, index - 2, first, count, steps) for index in indices], axis=0),
            jnp.concatenate(
                [k1[3 * a + b].reshape(3 * channels, channels) for a in steps for b in range(3)], axis=1
            ),
            (((1,), (1,)), ((), ())),
            preferred_element_type=jnp.float32,
        )
        return shifted(parts, channels)

    no_rows = {"inner": (), "near": (), "far": (no_z,), "outer": (both(no_z, zero), both(no_z, one))}

    def hidden(kind, indices, first, count, oldest=0, newest=2, before=None):
        total = hidden_sum(indices, first, count, range(oldest, newest + 1))
        if before is not None:
            total = total + before
        bias = jnp.concatenate([bias1[0], bias1[1]], axis=1)
        value = silu(total + bias)
        value = value.reshape(len(indices), count, columns, channels)
        for n, index in enumerate(indices):
            new = value[n]
            if no_rows[kind]:
                new = jnp.stack([jnp.where(no_rows[kind][row], 0.0, new[row]) for row in range(count)])
            h[index, pl.ds(first, count)] = new.astype(h.dtype)

    def inner(*indices, oldest=0):
        with jax.named_scope("inner" + "_".join(map(str, indices))):
            hidden("inner", indices, half * other, half, oldest)

    def outer(*indices, oldest=0):
        with jax.named_scope("outer" + "_".join(map(str, indices))):
            hidden("outer", indices, half * core, half, oldest)

    def near(*indices, oldest=0):
        with jax.named_scope("near" + "_".join(map(str, indices))):
            hidden("near", indices, 1 + core, 1, oldest)

    def far(*indices, oldest=0):
        with jax.named_scope("far" + "_".join(map(str, indices))):
            hidden("far", indices, (rows - 1) * core, 1, oldest)

    def outer_begin(index):
        with jax.named_scope("outer%da" % index):
            acc2[...] = hidden_sum((index,), half * core, half, range(1, 3))

    def outer_end(index):
        with jax.named_scope("outer%db" % index):
            hidden("outer", (index,), half * core, half, 0, 0, acc2[...])

    def second(index, first, count, steps, blocks):
        matrix = jnp.concatenate(
            [
                jnp.concatenate([k2[n, 3 * (a + shift) + b, e] for n, shift in blocks for e in range(3)], axis=1)
                for a in steps
                for b in range(3)
            ],
            axis=0,
        )
        parts = jnp.dot(taps(h, index, first, count, steps), matrix, preferred_element_type=jnp.float32)
        return [shifted(parts[:, 3 * k * width : 3 * (k + 1) * width], width) for k in range(len(blocks))]

    whole = ((0, 0), (1, 0))

    def share(slot, local):
        place = half * core + local
        return [
            remote(pieces.at[slot, 0], incoming.at[place], q_s, q_r.at[slot], next_same),
            remote(pieces.at[slot, 1], incoming.at[place], q_s, q_r.at[slot], next_cross),
        ]

    shares = [share(0, other), share(1, core)]

    def send_share(slot, local):
        with jax.named_scope("share%d" % slot):
            halves = second(frames, local, 1, range(0, 2), whole)
            for n in (1, 0):
                pieces[slot, n] = halves[n].astype(pieces.dtype)
            for condition, order in ((zero, (0, 1)), (one, (1, 0))):

                @pl.when(condition)
                def _():
                    for n in order:
                        shares[slot][n].start()


    result = [
        remote(going.at[t - 1], out.at[t, mine], o_s, o_r.at[t], peer) for t in range(1, frames // 2)
    ]
    part0 = remote(going0, sum0.at[mine], o_s, o_r.at[0], peer)

    def latent(t):
        with jax.named_scope("latent%d" % t):
            own, away = second(2 * t, 0, half, range(3), whole)
            going[t - 1] = silu(away + bias2[1]).astype(out.dtype).reshape(half, columns, width)
            result[t - 1].start()
            out[t, mine] = silu(own + bias2[0]).astype(out.dtype).reshape(half, columns, width)

    def later_steps(steps=range(1, 3), start=True):
        with jax.named_scope("latent1a%d" % len(steps)):
            halves = second(2, 0, half, steps, whole)
            for n in range(2):
                acc[n] = halves[n] if start else acc[n] + halves[n]

    def own_steps(first):
        place = pl.ds(half * core if first == 0 else half, half)
        with jax.named_scope("own1a"):
            acc[0] = second(2, first, half, range(1, 3), ((0, 0),))[0]
        with jax.named_scope("own"):
            one_sum, then = second(2, first, half, range(0, 1), ((0, 2), (0, 0)))
            sum0[place] = one_sum.reshape(half, columns, width)
            out[1, place] = silu(then + acc[0] + bias2[0]).astype(out.dtype).reshape(half, columns, width)

    def last_steps():
        with jax.named_scope("tailA"):
            first, then = second(2, 0, half, range(0, 1), ((1, 2), (1, 0)))
            going0[...] = first.reshape(half, columns, width)
            part0.start()
            going[0] = silu(then + acc[1] + bias2[1]).astype(out.dtype).reshape(half, columns, width)
            result[0].start()
        with jax.named_scope("tailB"):
            first, then = second(2, 0, half, range(0, 1), ((0, 2), (0, 0)))
            sum0[mine] = first.reshape(half, columns, width)
            out[1, mine] = silu(then + acc[0] + bias2[0]).astype(out.dtype).reshape(half, columns, width)

    def wait_z(which, copies):
        with jax.named_scope("zwait%d" % which):

            @pl.when(has_z)
            def _():
                copies[0][which].wait_recv()

    def pass_on(f, n):
        with jax.named_scope("pass%d%d" % (f, n)):
            x_in[f][n].wait_recv()
            condition, copy = forward_z[f][n]
            if (f, n) != (0, 0):
                pl.when(condition)(copy.start)
            if n == 0:
                forward_p[f].start()

    def from_peer(name, copy):
        @pl.when(zero)
        def _():
            with jax.named_scope(name):
                copy.wait_recv()

    def halo_ready(name, copy):
        with jax.named_scope(name):

            @pl.when(has_z)
            def _():
                copy.wait_recv()

    def w2_ready():
        with jax.named_scope("w2wait"):
            wait_bytes(k2, load.at[3])

    with jax.named_scope("w1wait"):
        remote(w1, k1.at[:, :, other], w_s, w1_r, peer).wait_recv()
        remote(b1, bias1.at[other], b_s.at[0], b_r.at[0], peer).wait_recv()
        to_peer[2].wait_recv()

    last = frames + 1

    @pl.when(both(one, has_next))
    def _():
        inner(frames, last)
        forward_h[2].start()

    @pl.when(both(one, no_next))
    def _():
        inner(frames)
        forward_h[3].start()

    @pl.when(both(one, no_prev))
    def _():
        inner(3, oldest=1)
        forward_h[1].start()
        inner(2, oldest=2)
        forward_h[0].start()

    @pl.when(both(one, has_next, above))
    def _():
        slanted.start()

    @pl.when(has_next)
    def _():
        w2_ready()
        from_peer("hwait2", forward_h[2])
        wait_z(0, z_full)
        near(frames, last)
        send_share(0, other)

        wait_z(1, z_full)

        @pl.when(jnp.logical_or(above, has_prev))
        def _():
            far(frames, last)
            send_share(1, core)

    def middle():
        for index in range(frames - 1, 3, -1):
            inner(index)
            outer(index)
        for t in range(2, frames // 2):
            latent(t)

    def own_last():
        @pl.when(no_next)
        def _():
            wait_z(0, z_short)
            wait_z(1, z_short)
            outer(frames)

    def own_ready():
        @pl.when(no_next)
        def _():
            w2_ready()
            from_peer("hwait2", forward_h[3])

    @pl.when(no_prev)
    def _():
        own_last()
        own_ready()
        middle()

        @pl.when(both(has_next, tile == 0))
        def _():
            far(frames, last)
            outer(3, oldest=1)
            outer(2, oldest=2)

        @pl.when(jnp.logical_or(above, no_next))
        def _():
            outer(3, oldest=1)
            outer(2, oldest=2)

        @pl.when(one)
        def _():
            rest_h[1].start()
            rest_h[0].start()

        @pl.when(both(has_next, tile == 0))
        def _():
            send_share(1, core)

        @pl.when(one)
        def _():
            own_steps(0)

        @pl.when(zero)
        def _():
            forward_h[1].wait_recv()
            forward_h[0].wait_recv()
            later_steps()
            last_steps()
            for copy in rest_h:
                copy.wait_recv()
            own_steps(half)

    @pl.when(has_prev)
    def _():
        @pl.when(one)
        def _():
            pass_on(1, 0)
            pass_on(1, 1)
            inner(3)
            forward_h[1].start()
            pass_on(0, 1)
            own_last()
            pass_on(0, 0)
            inner(2)
            forward_h[0].start()

        @pl.when(zero)
        def _():
            own_last()

        own_ready()
        middle()
        later_steps(range(2, 3))
        @pl.when(one)
        def _():
            halo_ready("fwait1", f_in[1])
            halo_ready("fwait0", f_in[0])
            outer(3)
            outer(2)
            later_steps(range(1, 2), False)
            last_steps()

        @pl.when(zero)
        def _():
            forward_p[1].wait_recv()
            halo_ready("fwait1", f_in[1])
            outer(3)
            forward_h[1].wait_recv()
            forward_p[0].wait_recv()
            forward_h[0].wait_recv()
            halo_ready("fwait0", f_in[0])
            outer(2)
            later_steps(range(1, 2), False)
            last_steps()


    takes = jnp.logical_or(has_prev, one)

    @pl.when(takes)
    def _():
        remote(going0, sum0.at[theirs], o_s, o_r.at[0], peer).wait_recv()

    def close(first, count, extra):
        total = sum0[pl.ds(first, count)].reshape(count * columns, width)
        if extra:
            total = total + incoming[pl.ds(first, count)].reshape(count * columns, width).astype(jnp.float32)
        out[0, pl.ds(first, count)] = silu(total + bias2[0]).astype(out.dtype).reshape(count, columns, width)

    @pl.when(has_prev)
    def _():
        for slot, pair in enumerate(((half - 1, half), (0, rows - 1))):
            with jax.named_scope("close%d" % slot):
                wait_bytes(pieces.at[0], q_r.at[slot])
                for row in pair:
                    close(row, 1, True)

    @pl.when(no_prev)
    def _():
        close(0, rows, False)

    with jax.named_scope("ends"):
        for copy in to_peer:
            copy.wait_send()
        for t in range(1, frames // 2):
            copy = remote(going.at[t - 1], out.at[t, theirs], o_s, o_r.at[t], peer)
            when(takes if t == 1 else None, copy.wait_recv)
        wait_bytes(v.at[pl.ds(0, frames // 2 + 1), low], o_s)

        @pl.when(has_next)
        def _():
            wait_bytes(incoming, q_s)

        @pl.when(both(one, has_next, tile == 0))
        def _():
            wait_bytes(v.at[pl.ds(0, BACK), pl.ds(0, rows)], x_s)

        @pl.when(both(one, has_next, above))
        def _():
            wait_bytes(v.at[pl.ds(0, BACK), pl.ds(0, rows + 1)], x_s)

        for condition, count in (
            (both(no_prev, has_next), 4), (both(no_prev, no_next), 3),
            (both(has_prev, has_next), 6), (both(has_prev, no_next), 5),
        ):

            @pl.when(both(one, condition))
            def _():
                wait_bytes(v.at[pl.ds(0, count), low], p_s)

        for side, condition in ((0, above), (1, below)):
            forwards = both(one, condition)
            for after, count in ((has_next, frames), (no_next, frames - 1)):
                if side == 0:

                    @pl.when(both(zero, condition, after))
                    def _():
                        wait_bytes(v.at[pl.ds(0, count), low], z_s[0])

                else:

                    @pl.when(both(forwards, after, no_prev))
                    def _():
                        wait_bytes(v.at[pl.ds(0, count), low], z_s[1])

                    @pl.when(both(forwards, after, has_prev))
                    def _():
                        wait_bytes(v.at[pl.ds(0, count + BACK), low], z_s[1])

            if side == 0:

                @pl.when(both(forwards, has_prev))
                def _():
                    wait_bytes(v.at[pl.ds(0, 1), low], z_s[0])


def shards(tiles, slabs, video, first_weight, first_bias, second_weight, second_bias):
    frames, rows, columns, channels = video.shape
    half = rows // 2
    assert half == 2 and first_weight.shape[3] == channels == second_bias.shape[0] and frames >= 4 and frames % 2 == 0
    part = first_bias.shape[0]
    width = second_bias.shape[0]
    anywhere = pl.BlockSpec(memory_space=pltpu.HBM)
    inside = pl.BlockSpec(memory_space=pltpu.VMEM)
    dma = pltpu.SemaphoreType.DMA
    vmem = pltpu.VMEM
    latents = frames // 2
    return pl.pallas_call(
        functools.partial(kernel, tiles, slabs),
        out_shape=jax.ShapeDtypeStruct((latents, rows, columns, width), jnp.bfloat16),
        in_specs=[anywhere] * 5,
        out_specs=inside,
        scratch_shapes=[
            vmem((BACK + frames, rows + 2, columns, channels), jnp.bfloat16),
            vmem((frames + 2, half + 4, columns, channels), jnp.bfloat16),
            vmem((9, 3, 2, part, channels), jnp.bfloat16),
            vmem((2, 9, 3, channels, width), jnp.bfloat16),
            vmem((2, 1, part), jnp.float32),
            vmem((2, 1, width), jnp.float32),
            vmem((2, 2, columns, width), jnp.bfloat16),
            vmem((rows, columns, width), jnp.bfloat16),
            vmem((latents - 1, half, columns, width), jnp.bfloat16),
            vmem((half, columns, width), jnp.float32),
            vmem((rows, columns, width), jnp.float32),
            vmem((2, half * columns, width), jnp.float32),
            vmem((half * columns, channels), jnp.float32),
            dma((5,)), dma, dma((2,)), dma, dma, dma((2,)), dma((2 * BACK + 1,)), dma((2,)), dma((BACK,)), dma((2,)),
            dma((latents,)),
        ],
        compiler_params=pltpu.CompilerParams(
            collective_id=0, has_side_effects=True, vmem_limit_bytes=32 << 20
        ),
    )(
        *(
            pltpu.with_memory_space_constraint(operand, pltpu.HBM)
            for operand in (
                video,
                jnp.swapaxes(first_weight, 3, 4).reshape(9, 3, part, channels),
                first_bias.reshape(1, part),
                second_weight.reshape(9, 3, channels, 2 * width),
                second_bias.reshape(1, width),
            )
        )
    )


def solution(mesh):
    placed = (
        P(("clip", "slab"), "tile", None, None),
        P(None, None, None, None, "chan"),
        P("chan"),
        P(),
        P("chan"),
    )
    return jax.shard_map(
        functools.partial(shards, mesh.shape["tile"], mesh.shape["slab"]),
        mesh=mesh,
        in_specs=placed,
        out_specs=P(("clip", "slab"), "tile", None, "chan"),
        check_vma=False,
    )
```
